32 devices in a mesh: layer: 8 (over z, y), latent: 4 (over x, core).
Axes of the slice: x: 2, y: 2, z: 4, core: 2. Of those that a mesh axis runs over, the one named last changes fastest.
Arguments:
- layer_inputs: bfloat16 [384, 8192], P('latent', 'layer'), may hold values from -6 to 6
- mlp_outputs: bfloat16 [384, 8192], P('latent', 'layer'), may hold values from -6 to 6
- enc_weight: bfloat16 [8192, 4096], P('layer', 'latent'), may hold values from -0.125 to 0.125
- enc_bias: float32 [4, 4096], P(None, 'latent'), may hold values from -1 to 0.5
- dec_weight: bfloat16 [4, 4096, 8192], P(None, 'latent', 'layer'), may hold values from -0.046875 to 0.046875
Outputs:
- enc_grad: float32 [8192, 4096], P('layer', 'latent')
- dec_grad: bfloat16 [4, 4096, 8192], P(None, 'latent', 'layer')
The draws below stay inside these ranges and needn't reach their ends.
All inputs are finite; a program needn't handle non-finite values.
Results may differ from the reference program's by a relative error of at most 0.011.
Values may be sent and summed in bfloat16 or wider, within the bound.
A program may use at most 64 MiB of HBM per device.

```python
import jax
import jax.numpy as jnp
from jax import lax

D = 2048
F = 4096
ROWS = 384
LAYERS = 4


def level_of(rng, extent, pieces, low, largest):
    def one(dim, blocks):
        steps = jax.random.uniform(jax.random.fold_in(jax.random.fold_in(rng, 6), dim), (blocks,), jnp.float32, low / len(pieces), largest / len(pieces))
        return jnp.repeat(jnp.exp(steps), extent[dim] // blocks).reshape((-1,) + (1,) * (len(extent) - dim - 1))

    loudness = one(*pieces[0])
    for cut in pieces[1:]:
        loudness = loudness * one(*cut)
    return loudness


def gaussian(rng, extent, deviation, most, pieces=(), held_as=jnp.bfloat16):
    gain = level_of(rng, extent, pieces, -0.22, 0.18) if pieces else 1.0
    values = jax.random.normal(rng, extent, jnp.float32) * deviation * gain
    return jnp.minimum(jnp.maximum(values, -most), most).astype(held_as)


def setup_inputs(seed: int = 0) -> dict:
    key_of = jax.random.split(jax.random.key(seed), 6)
    return {
        "layer_inputs": gaussian(key_of[0], (ROWS, LAYERS * D), 1.0, 6.0, ((0, 4), (1, 8))),
        "mlp_outputs": gaussian(key_of[1], (ROWS, LAYERS * D), 1.0, 6.0, ((0, 4), (1, 8))),
        "enc_weight": gaussian(key_of[2], (LAYERS * D, F), D ** -0.5, 0.125, ((0, 8), (1, 4))),
        "enc_bias": jnp.clip(-1.0 + 1.5 * jax.random.uniform(key_of[3], (LAYERS, F), jnp.float32) ** level_of(key_of[3], (LAYERS, F), ((1, 4),), -0.2, 0.2), -1.0, 0.5),
        "dec_weight": gaussian(key_of[4], (LAYERS, F, LAYERS * D), (LAYERS * F) ** -0.5, 0.046875, ((1, 4), (2, 8))),
    }


def reference(layer_inputs, mlp_outputs, enc_weight, enc_bias, dec_weight):
    rscale = ROWS ** -0.5
    pre_list = []
    latent_list = []
    for source in range(LAYERS):
        layer_in = layer_inputs[:, source * D:(source + 1) * D]
        pre_acts = jnp.dot(layer_in, enc_weight[source * D:(source + 1) * D], preferred_element_type=jnp.float32) + enc_bias[source][None, :]
        pre_list.append(pre_acts)
        latent_list.append(jnp.maximum(pre_acts, 0.0).astype(jnp.bfloat16))
    grad_list = []
    for target in range(LAYERS):
        recon = jnp.zeros((ROWS, D), jnp.float32)
        for source in range(target + 1):
            recon = recon + jnp.dot(latent_list[source], dec_weight[source, :, target * D:(target + 1) * D], preferred_element_type=jnp.float32)
        wanted = mlp_outputs[:, target * D:(target + 1) * D].astype(jnp.float32)
        grad_list.append(((recon - wanted) * rscale).astype(jnp.bfloat16))
    dec_rows = []
    enc_rows = []
    for source in range(LAYERS):
        blocks = []
        lat_grad = jnp.zeros((ROWS, F), jnp.float32)
        for target in range(LAYERS):
            if target >= source:
                piece = lax.dot_general(latent_list[source], grad_list[target], (((0,), (0,)), ((), ())), preferred_element_type=jnp.float32)
                blocks.append(piece.astype(jnp.bfloat16))
                weight = dec_weight[source, :, target * D:(target + 1) * D]
                lat_grad = lat_grad + lax.dot_general(grad_list[target], weight, (((1,), (1,)), ((), ())), preferred_element_type=jnp.float32)
            else:
                blocks.append(jnp.zeros((F, D), jnp.bfloat16))
        dec_rows.append(jnp.concatenate(blocks, axis=1))
        pre_grad = jnp.where(pre_list[source] > 0.0, lat_grad, 0.0).astype(jnp.bfloat16)
        layer_in = layer_inputs[:, source * D:(source + 1) * D]
        enc_rows.append(lax.dot_general(layer_in, pre_grad, (((0,), (0,)), ((), ())), preferred_element_type=jnp.float32))
    return jnp.concatenate(enc_rows, axis=0), jnp.stack(dec_rows, axis=0)
```

```python
import functools

import jax
import jax.numpy as jnp
from jax import lax
from jax.experimental import pallas as pl
from jax.experimental.pallas import tpu as pltpu
from jax.sharding import PartitionSpec as P

MESH = pl.DeviceIdType.MESH
F32 = jnp.float32
BF16 = jnp.bfloat16
CHUNKS = (6, 3, 2)


def exchange_kernel(
    layers, blocks, chunks, rscale,
    x_hbm, mlp_hbm, w_hbm, bias_hbm, v_hbm,
    dec_out, xg_out, pg_out,
    xg, mlp, w, bias_all, v, pre, his, hir, los, lor, lat, recon, rss, rsr, og, acc, zds, zdr, ys, yr, pg, dec,
    x_ss, x_rs, hi_ss, hi_rs, lo_ss, lo_rs, zu_ss, zu_rs, rs_ss, rs_rs, og_ss, og_rs, zd_ss, zd_rs, y_ss, y_rs,
    own_sem, in_sem, dec_sem, out_sem,
):
    p = lax.axis_index("layer")
    q = lax.axis_index("latent")
    t = p // 2
    y = p % 2
    n = chunks
    top = layers - 1
    last = t == top
    below = t < top
    s = x_hbm.shape[0] // n
    size = s * blocks
    half = w.shape[1] // 2
    partner = (p + 1 - 2 * y, q)
    up = (p + 2, q)
    down = (p - 2, q)
    chips = blocks // 2

    def blk(k):
        return ((q // 2 + k // 2) % chips) * 2 + (q % 2 + k % 2) % 2

    def span(j):
        return pl.ds(pl.multiple_of(j * size, size), size)

    def piece(j, b):
        return pl.ds(pl.multiple_of(j * size + b * s, s), s)

    def mine(j):
        return pl.ds(pl.multiple_of(j * s, s), s)

    def rcopy(src, dst, ss, rs, dev):
        return pltpu.make_async_remote_copy(
            src_ref=src, dst_ref=dst, send_sem=ss, recv_sem=rs, device_id=dev, device_id_type=MESH
        )

    def loop(lower, upper, step):
        def body(i, carry):
            step(i)
            return carry

        lax.fori_loop(lower, upper, body, 0)

    def own_x(j):
        return pltpu.make_async_copy(x_hbm.at[mine(j)], xg.at[piece(j, q)], own_sem.at[j])

    w_copy = pltpu.make_async_copy(w_hbm, w, in_sem.at[0])
    bias_copy = pltpu.make_async_copy(bias_hbm, bias_all, in_sem.at[1])
    mlp_copy = pltpu.make_async_copy(mlp_hbm, mlp, in_sem.at[2])
    v_copy = pltpu.make_async_copy(v_hbm, v, in_sem.at[3])
    for j in range(n):
        own_x(j).start()
    for copy in (w_copy, bias_copy, mlp_copy, v_copy):
        copy.start()

    barrier = pltpu.get_barrier_semaphore()
    for k in range(1, blocks):
        pl.semaphore_signal(barrier, inc=1, device_id=(p, blk(k)), device_id_type=MESH)
    pl.semaphore_signal(barrier, inc=1, device_id=partner, device_id_type=MESH)

    @pl.when(below)
    def _():
        pl.semaphore_signal(barrier, inc=1, device_id=up, device_id_type=MESH)

    @pl.when(t > 0)
    def _():
        pl.semaphore_signal(barrier, inc=1, device_id=down, device_id_type=MESH)

    neighbours = blocks + below.astype(jnp.int32) + (t > 0).astype(jnp.int32)
    pl.semaphore_wait(barrier, neighbours)

    others = list(range(2, blocks)) + [1]

    def x_copy(j, k):
        return rcopy(x_hbm.at[mine(j)], xg.at[piece(j, q)], x_ss.at[j, k], x_rs.at[j, q], (p, blk(k)))

    def x_in(j, k):
        b = blk(k)
        return rcopy(x_hbm.at[mine(j)], xg.at[piece(j, b)], x_ss.at[j, k], x_rs.at[j, b], (p, b))

    def send_x(j):
        for k in others:
            x_copy(j, k).start()

    loop(0, n, send_x)

    def hi_copy(j):
        return rcopy(his.at[span(j)], hir.at[span(j)], hi_ss.at[j], hi_rs.at[j], partner)

    def lo_copy(j):
        return rcopy(los.at[span(j)], lor.at[span(j)], lo_ss.at[j], lo_rs.at[j], partner)

    def encode(j):
        own_x(j).wait()
        for k in others:
            x_in(j, k).wait_recv()
        part = jnp.dot(xg[span(j), :], w[...], preferred_element_type=F32)
        pre[span(j), :] = part
        hi = part.astype(BF16)
        his[span(j), :] = hi
        hi_copy(j).start()
        los[span(j), :] = (part - hi.astype(F32)).astype(BF16)

    def zu_copy(l, j):
        part = lat.at[l, :, span(j)]
        return rcopy(part, part, zu_ss.at[l, j], zu_rs.at[l, j], up)

    bias_copy.wait()
    own_row = lax.broadcasted_iota(jnp.int32, bias_all.shape, 0) == t
    bias = jnp.sum(jnp.where(own_row, bias_all[...], 0.0), axis=0, keepdims=True)
    w_copy.wait()
    ahead = min(n, 2)
    loop(0, ahead, encode)

    def decoded(l, j):
        return jnp.dot(lat[l, 0, span(j)], v[l, :half, :], preferred_element_type=F32) + jnp.dot(
            lat[l, 1, span(j)], v[l, half:, :], preferred_element_type=F32
        )

    def own_latents(j):
        hi_copy(j).wait_recv()
        total = pre[span(j), :] + hir[span(j), :].astype(F32) + bias
        pre[span(j), :] = total
        value = jnp.maximum(total, 0.0).astype(BF16)
        lat[t, 0, span(j)] = value[:, :half]
        lat[t, 1, span(j)] = value[:, half:]

        @pl.when(below)
        def _():
            zu_copy(t, j).start()

        recon[span(j), :] = decoded(t, j)
        lo_copy(j).start()

    def relay(l, j):
        zu_copy(l, j).wait_recv()

        @pl.when(below)
        def _():
            zu_copy(l, j).start()

        recon[span(j), :] += decoded(l, j)

    def rs_copy(j, k):
        b = blk(k)
        return rcopy(rss.at[piece(j, b)], rsr.at[q, mine(j)], rs_ss.at[j, k], rs_rs.at[j, q], (p, b))

    def rs_in(j, k):
        b = blk(k)
        return rcopy(rss.at[piece(j, b)], rsr.at[b, mine(j)], rs_ss.at[j, k], rs_rs.at[j, b], (p, b))

    def send_sums(j):
        rss[span(j), :] = recon[span(j), :].astype(BF16)
        for k in others:
            rs_copy(j, k).start()

    def og_copy(j, k):
        part = og.at[piece(j, q)]
        return rcopy(part, part, og_ss.at[j, k], og_rs.at[j, q], (p, blk(k)))

    def og_in(j, k):
        b = blk(k)
        part = og.at[piece(j, b)]
        return rcopy(part, part, og_ss.at[j, k], og_rs.at[j, b], (p, b))

    def own_grad(j):
        total = recon[piece(j, q), :]
        for k in range(1, blocks):
            rs_in(j, k).wait_recv()
            total = total + rsr[blk(k), mine(j)].astype(F32)
        og[piece(j, q), :] = ((total - mlp[mine(j), :].astype(F32)) * rscale).astype(BF16)
        for k in others:
            og_copy(j, k).start()

    def zd_copy(l, j):
        return rcopy(zds.at[l, :, span(j)], zdr.at[l, :, span(j)], zd_ss.at[l, j], zd_rs.at[l, j], down)

    def y_copy(j):
        return rcopy(ys.at[:, span(j)], yr.at[:, span(j)], y_ss.at[j], y_rs.at[j], partner)

    def back(l, j, h):
        return lax.dot_general(
            og[span(j), :], v[l, h * half:(h + 1) * half, :], (((1,), (1,)), ((), ())), preferred_element_type=F32
        )

    def backward(j):
        for k in range(1, blocks):
            og_in(j, k).wait_recv()

        def produce(l):
            for h in range(2):
                acc[l, h, span(j)] = back(l, j, h)

            @pl.when(last)
            def _():
                pass_on(l, j)

        loop(0, t + 1, produce)

    def pass_on(l, j):
        @pl.when(l < t)
        def _():
            for h in range(2):
                zds[l, h, span(j)] = acc[l, h, span(j)].astype(BF16)
            zd_copy(l, j).start()

        @pl.when(l == t)
        def _():
            for h in range(2):
                ys[h, span(j)] = acc[l, h, span(j)].astype(BF16)
            y_copy(j).start()

    def combine(j):
        def add(l):
            zd_copy(l, j).wait_recv()
            for h in range(2):
                acc[l, h, span(j)] += zdr[l, h, span(j)].astype(F32)
            pass_on(l, j)

        loop(0, t + 1, add)

    def masked(j):
        y_copy(j).wait_recv()
        lo_copy(j).wait_recv()
        active = pre[span(j), :] + lor[span(j), :].astype(F32) > 0.0
        for h in range(2):
            total = acc[t, h, span(j)] + yr[h, span(j)].astype(F32)
            side = slice(h * half, (h + 1) * half)
            pg[span(j), side] = jnp.where(active[:, side], total, 0.0).astype(BF16)

    def dec_copy(l):
        return pltpu.make_async_copy(dec.at[l], dec_out.at[l], dec_sem.at[l])

    def dec_piece(l):
        for h in range(2):
            part = lax.dot_general(lat[l, h], og[...], (((0,), (0,)), ((), ())), preferred_element_type=F32)
            dec[l, h * half:(h + 1) * half, :] = part.astype(BF16)
        dec_copy(l).start()

    def blank(l):
        dec[l] = jnp.zeros((2 * half, dec.shape[2]), BF16)
        dec_copy(l).start()

    near = t == top - 1
    grad_lag = jnp.where(last, 1, 2)
    back_lag = jnp.where(last, 1, 3)
    sum_lag = jnp.where(last, 1, jnp.where(near, 3, max(n, 3)))
    dec_at = n + sum_lag - below.astype(jnp.int32)
    v_copy.wait()
    mlp_copy.wait()

    def step(i):
        live = i < n

        @pl.when(i + ahead < n)
        def _():
            encode(i + ahead)

        @pl.when(live)
        def _():
            own_latents(i)

        @pl.when(jnp.logical_and(live, t > 0))
        def _():
            relay(t - 1, i)

        j = i - grad_lag

        @pl.when(jnp.logical_and(j >= 0, j < n))
        def _():
            own_grad(j)

        @pl.when(live)
        def _():
            loop(2, t, lambda d: relay(t - d, i))

        j2 = i - back_lag

        @pl.when(jnp.logical_and(j2 >= 0, j2 < n))
        def _():
            backward(j2)

        @pl.when(jnp.logical_and(live, t > 1))
        def _():
            relay(0, i)

        @pl.when(live)
        def _():
            send_sums(i)

        @pl.when(i == dec_at)
        def _():
            loop(0, t + 1, dec_piece)

        j3 = i - sum_lag

        @pl.when(jnp.logical_and(below, jnp.logical_and(j3 >= 0, j3 < n)))
        def _():
            combine(j3)

        @pl.when(jnp.logical_and(j3 >= 1, j3 <= n))
        def _():
            masked(j3 - 1)

    loop(t + 1, layers, blank)
    loop(0, n + sum_lag + 1, step)

    pg_copy = pltpu.make_async_copy(pg, pg_out, out_sem.at[0])
    xg_copy = pltpu.make_async_copy(xg, xg_out, out_sem.at[1])
    pg_copy.start()
    xg_copy.start()

    def drain(j):
        for k in range(1, blocks):
            x_copy(j, k).wait_send()
            rs_copy(j, k).wait_send()
            og_copy(j, k).wait_send()
        hi_copy(j).wait_send()
        lo_copy(j).wait_send()
        y_copy(j).wait_send()

        def passed(l):
            @pl.when(below)
            def _():
                zu_copy(l, j).wait_send()

            @pl.when(l < t)
            def _():
                zd_copy(l, j).wait_send()

        loop(0, t + 1, passed)

    loop(0, n, drain)
    for l in range(layers):
        dec_copy(l).wait()
    pg_copy.wait()
    xg_copy.wait()


def exchange(layer_inputs, mlp_outputs, enc_weight, enc_bias, dec_weight):
    layers, latents, width = dec_weight.shape
    blocks = lax.axis_size("latent")
    rb, depth = layer_inputs.shape
    rows = rb * blocks
    half = latents // 2
    rscale = rows ** (-0.5)
    chunks = next((c for c in CHUNKS if rb % (16 * c) == 0), 1)
    hbm = pl.BlockSpec(memory_space=pltpu.HBM)
    dma = pltpu.SemaphoreType.DMA
    per_chunk = dma((chunks,))
    per_block = dma((chunks, blocks))
    per_layer = dma((layers, chunks))
    whole = pltpu.VMEM((rows, latents), BF16)
    sides = pltpu.VMEM((2, rows, half), BF16)
    sent = pltpu.VMEM((layers, 2, rows, half), BF16)
    return pl.pallas_call(
        functools.partial(exchange_kernel, layers, blocks, chunks, rscale),
        out_shape=(
            jax.ShapeDtypeStruct((layers, latents, width), BF16),
            jax.ShapeDtypeStruct((rows, depth), BF16),
            jax.ShapeDtypeStruct((rows, latents), BF16),
        ),
        in_specs=[hbm] * 5,
        out_specs=(pl.BlockSpec(memory_space=pl.ANY),) * 3,
        scratch_shapes=[
            pltpu.VMEM((rows, depth), BF16),
            pltpu.VMEM((rb, width), BF16),
            pltpu.VMEM((depth, latents), BF16),
            pltpu.VMEM((layers, latents), F32),
            pltpu.VMEM((layers, latents, width), BF16),
            pltpu.VMEM((rows, latents), F32),
            whole, whole, whole, whole,
            sent,
            pltpu.VMEM((rows, width), F32),
            pltpu.VMEM((rows, width), BF16),
            pltpu.VMEM((blocks, rb, width), BF16),
            pltpu.VMEM((rows, width), BF16),
            pltpu.VMEM((layers, 2, rows, half), F32),
            sent, sent, sides, sides, whole,
            pltpu.VMEM((layers, latents, width), BF16),
            per_block, per_block, per_chunk, per_chunk, per_chunk, per_chunk, per_layer, per_layer,
            per_block, per_block, per_block, per_block, per_layer, per_layer, per_chunk, per_chunk,
            per_chunk, dma((4,)), dma((layers,)), dma((2,)),
        ],
        compiler_params=pltpu.CompilerParams(
            collective_id=0, has_side_effects=True, vmem_limit_bytes=56 * 2**20
        ),
        name="exchange",
    )(layer_inputs, mlp_outputs, enc_weight, enc_bias, dec_weight)


def finish_kernel(
    xg_hbm, pg_hbm, dec_hbm, enc_out, dec_out, xg, pg, enc, dec, in_sem, dec_in, dec_sem, enc_sem
):
    layers = dec.shape[0]
    piece = enc.shape[0] // layers
    ins = [
        pltpu.make_async_copy(xg_hbm, xg, in_sem.at[0]),
        pltpu.make_async_copy(pg_hbm, pg, in_sem.at[1]),
    ]
    reads = [pltpu.make_async_copy(dec_hbm.at[l], dec.at[l], dec_in.at[l]) for l in range(layers)]
    for copy in ins + reads:
        copy.start()
    for copy in ins:
        copy.wait()
    writes = []
    for l in range(layers):
        part = pl.ds(l * piece, piece)
        enc[part, :] = lax.dot_general(
            xg[:, part], pg[...], (((0,), (0,)), ((), ())), preferred_element_type=F32
        )
        writes.append(pltpu.make_async_copy(enc.at[part], enc_out.at[part], enc_sem.at[l]))
        writes[-1].start()
        reads[l].wait()
        writes.append(pltpu.make_async_copy(dec.at[l], dec_out.at[l], dec_sem.at[l]))
        writes[-1].start()
    for copy in writes:
        copy.wait()


def local(layer_inputs, mlp_outputs, enc_weight, enc_bias, dec_weight):
    dec, xg, pg = exchange(layer_inputs, mlp_outputs, enc_weight, enc_bias, dec_weight)
    hbm = pl.BlockSpec(memory_space=pltpu.HBM)
    per_layer = pltpu.SemaphoreType.DMA((dec.shape[0],))
    return pl.pallas_call(
        finish_kernel,
        in_specs=[hbm] * 3,
        out_specs=(hbm,) * 2,
        out_shape=(
            jax.ShapeDtypeStruct(enc_weight.shape, F32),
            jax.ShapeDtypeStruct(dec_weight.shape, BF16),
        ),
        scratch_shapes=[
            pltpu.VMEM(xg.shape, BF16),
            pltpu.VMEM(pg.shape, BF16),
            pltpu.VMEM(enc_weight.shape, F32),
            pltpu.VMEM(dec.shape, BF16),
            pltpu.SemaphoreType.DMA((2,)),
            per_layer, per_layer, per_layer,
        ],
        compiler_params=pltpu.CompilerParams(vmem_limit_bytes=56 * 2**20),
        name="finish",
    )(xg, pg, dec)


def solution(mesh):
    in_specs = (
        P("latent", "layer"),
        P("latent", "layer"),
        P("layer", "latent"),
        P(None, "latent"),
        P(None, "latent", "layer"),
    )
    out_specs = (P("layer", "latent"), P(None, "latent", "layer"))
    return jax.shard_map(local, mesh=mesh, in_specs=in_specs, out_specs=out_specs, check_vma=False)
```

```python
import functools

import jax
import jax.numpy as jnp
from jax import lax
from jax.experimental import pallas as pl
from jax.experimental.pallas import tpu as pltpu
from jax.sharding import PartitionSpec as P

MESH = pl.DeviceIdType.MESH
F32 = jnp.float32
BF16 = jnp.bfloat16
CHUNKS = (6, 3, 2)
NEAR = 5


def exchange_kernel(
    layers, blocks, chunks, rscale,
    x_hbm, mlp_hbm, w_hbm, bias_hbm, v_hbm,
    dec, xg, pg,
    mlp, w, bias_all, v, pre, his, hir, los, lor, lat, recon, rss, rsr, og, acc, zds, zdr, ys, yr,
    x_ss, x_rs, hi_ss, hi_rs, lo_ss, lo_rs, zu_ss, zu_rs, rs_ss, rs_rs, og_ss, og_rs, zd_ss, zd_rs, y_ss, y_rs,
    own_sem, in_sem,
):
    p = lax.axis_index("layer")
    q = lax.axis_index("latent")
    t = p // 2
    y = p % 2
    n = chunks
    top = layers - 1
    last = t == top
    below = t < top
    s = x_hbm.shape[0] // n
    size = s * blocks
    half = w.shape[1] // 2
    partner = (p + 1 - 2 * y, q)
    up = (p + 2, q)
    down = (p - 2, q)
    chips = blocks // 2

    def blk(k):
        return ((q // 2 + k // 2) % chips) * 2 + (q % 2 + k % 2) % 2

    def span(j):
        return pl.ds(pl.multiple_of(j * size, size), size)

    def piece(j, b):
        return pl.ds(pl.multiple_of(j * size + b * s, s), s)

    def mine(j):
        return pl.ds(pl.multiple_of(j * s, s), s)

    def rcopy(src, dst, ss, rs, dev):
        return pltpu.make_async_remote_copy(
            src_ref=src, dst_ref=dst, send_sem=ss, recv_sem=rs, device_id=dev, device_id_type=MESH
        )

    def loop(lower, upper, step):
        def body(i, carry):
            step(i)
            return carry

        lax.fori_loop(lower, upper, body, 0)

    def own_x(j):
        return pltpu.make_async_copy(x_hbm.at[mine(j)], xg.at[piece(j, q)], own_sem.at[j])

    w_copy = pltpu.make_async_copy(w_hbm, w, in_sem.at[0])
    bias_copy = pltpu.make_async_copy(bias_hbm, bias_all, in_sem.at[1])
    mlp_copy = pltpu.make_async_copy(mlp_hbm, mlp, in_sem.at[2])
    v_copy = pltpu.make_async_copy(v_hbm, v, in_sem.at[3])
    for j in range(n):
        own_x(j).start()
    for copy in (w_copy, bias_copy, mlp_copy, v_copy):
        copy.start()

    barrier = pltpu.get_barrier_semaphore()
    for k in range(1, blocks):
        pl.semaphore_signal(barrier, inc=1, device_id=(p, blk(k)), device_id_type=MESH)
    pl.semaphore_signal(barrier, inc=1, device_id=partner, device_id_type=MESH)

    @pl.when(below)
    def _():
        pl.semaphore_signal(barrier, inc=1, device_id=up, device_id_type=MESH)

    @pl.when(t > 0)
    def _():
        pl.semaphore_signal(barrier, inc=1, device_id=down, device_id_type=MESH)

    neighbours = blocks + below.astype(jnp.int32) + (t > 0).astype(jnp.int32)
    pl.semaphore_wait(barrier, neighbours)

    others = list(range(2, blocks)) + [1]

    def x_copy(j, k):
        return rcopy(x_hbm.at[mine(j)], xg.at[piece(j, q)], x_ss.at[j, k], x_rs.at[j, q], (p, blk(k)))

    def x_in(j, k):
        b = blk(k)
        return rcopy(x_hbm.at[mine(j)], xg.at[piece(j, b)], x_ss.at[j, k], x_rs.at[j, b], (p, b))

    def send_x(j):
        for k in others:
            x_copy(j, k).start()

    loop(0, n, send_x)

    def side(h):
        return slice(h * half, (h + 1) * half)

    def hi_copy(j, h):
        return rcopy(his.at[h, span(j)], hir.at[h, span(j)], hi_ss.at[j, h], hi_rs.at[j, h], partner)

    def lo_copy(j):
        return rcopy(los.at[:, span(j)], lor.at[:, span(j)], lo_ss.at[j], lo_rs.at[j], partner)

    def encode(j):
        own_x(j).wait()
        for k in others:
            x_in(j, k).wait_recv()
        for h in range(2):
            part = jnp.dot(xg[span(j), :], w[:, side(h)], preferred_element_type=F32)
            pre[h, span(j)] = part
            hi = part.astype(BF16)
            his[h, span(j)] = hi
            hi_copy(j, h).start()
            los[h, span(j)] = (part - hi.astype(F32)).astype(BF16)

    def zu_copy(l, j, h):
        part = lat.at[l, h, span(j)]
        return rcopy(part, part, zu_ss.at[l, j, h], zu_rs.at[l, j, h], up)

    bias_copy.wait()
    own_row = lax.broadcasted_iota(jnp.int32, bias_all.shape, 0) == t
    bias = jnp.sum(jnp.where(own_row, bias_all[...], 0.0), axis=0, keepdims=True)
    w_copy.wait()
    ahead = min(n, 3)
    early = min(n, 2)
    loop(0, early, encode)

    def decoded(l, j):
        return jnp.dot(lat[l, 0, span(j)], v[l, :half, :], preferred_element_type=F32) + jnp.dot(
            lat[l, 1, span(j)], v[l, half:, :], preferred_element_type=F32
        )

    def own_latents(j):
        for h in range(2):
            hi_copy(j, h).wait_recv()
            total = pre[h, span(j)] + hir[h, span(j)].astype(F32) + bias[:, side(h)]
            pre[h, span(j)] = total
            lat[t, h, span(j)] = jnp.maximum(total, 0.0).astype(BF16)

            @pl.when(below)
            def _():
                zu_copy(t, j, h).start()

        lo_copy(j).start()

    def relay(l, j):
        for h in range(2):
            zu_copy(l, j, h).wait_recv()

            @pl.when(below)
            def _():
                zu_copy(l, j, h).start()

        recon[span(j), :] += decoded(l, j)

    def rs_copy(j, k):
        b = blk(k)
        return rcopy(rss.at[piece(j, b)], rsr.at[q, mine(j)], rs_ss.at[j, k], rs_rs.at[j, q], (p, b))

    def rs_in(j, k):
        b = blk(k)
        return rcopy(rss.at[piece(j, b)], rsr.at[b, mine(j)], rs_ss.at[j, k], rs_rs.at[j, b], (p, b))

    def send_sums(j):
        rss[span(j), :] = recon[span(j), :].astype(BF16)
        for k in others:
            rs_copy(j, k).start()

    def og_copy(j, k):
        part = og.at[piece(j, q)]
        return rcopy(part, part, og_ss.at[j, k], og_rs.at[j, q], (p, blk(k)))

    def og_in(j, k):
        b = blk(k)
        part = og.at[piece(j, b)]
        return rcopy(part, part, og_ss.at[j, k], og_rs.at[j, b], (p, b))

    def own_grad(j):
        total = recon[piece(j, q), :]
        for k in range(1, blocks):
            rs_in(j, k).wait_recv()
            total = total + rsr[blk(k), mine(j)].astype(F32)
        og[piece(j, q), :] = ((total - mlp[mine(j), :].astype(F32)) * rscale).astype(BF16)
        for k in others:
            og_copy(j, k).start()

    def zd_copy(l, j, h):
        return rcopy(zds.at[l, h, span(j)], zdr.at[l, h, span(j)], zd_ss.at[l, j, h], zd_rs.at[l, j, h], down)

    def y_copy(j, h):
        return rcopy(ys.at[h, span(j)], yr.at[h, span(j)], y_ss.at[j, h], y_rs.at[j, h], partner)

    def back(l, j, h):
        return lax.dot_general(
            og[span(j), :], v[l, h * half:(h + 1) * half, :], (((1,), (1,)), ((), ())), preferred_element_type=F32
        )

    def backward(j):
        for k in range(1, blocks):
            og_in(j, k).wait_recv()

        def produce(l):
            for h in range(2):
                acc[l, h, span(j)] = back(l, j, h)

                @pl.when(last)
                def _():
                    pass_on(l, j, h)

        loop(0, t + 1, produce)

    def pass_on(l, j, h):
        @pl.when(l < t)
        def _():
            zds[l, h, span(j)] = acc[l, h, span(j)].astype(BF16)
            zd_copy(l, j, h).start()

        @pl.when(l == t)
        def _():
            ys[h, span(j)] = acc[l, h, span(j)].astype(BF16)
            y_copy(j, h).start()

    def combine(j):
        def add(l):
            for h in range(2):
                zd_copy(l, j, h).wait_recv()
                acc[l, h, span(j)] += zdr[l, h, span(j)].astype(F32)
                pass_on(l, j, h)

            @pl.when(j == n - 1)
            def _():
                dec_piece(l)

        loop(0, t + 1, add)

    def masked(j):
        lo_copy(j).wait_recv()
        for h in range(2):
            y_copy(j, h).wait_recv()
            active = pre[h, span(j)] + lor[h, span(j)].astype(F32) > 0.0
            total = acc[t, h, span(j)] + yr[h, span(j)].astype(F32)
            pg[span(j), side(h)] = jnp.where(active, total, 0.0).astype(BF16)

    def dec_piece(l):
        for h in range(2):
            part = lax.dot_general(lat[l, h], og[...], (((0,), (0,)), ((), ())), preferred_element_type=F32)
            dec[l, h * half:(h + 1) * half, :] = part.astype(BF16)

    def blank(l):
        dec[l] = jnp.zeros((2 * half, dec.shape[2]), BF16)

    near = t == top - 1
    grad_lag = jnp.where(last, 1, 2)
    back_lag = jnp.where(last, 1, 3)
    sum_lag = jnp.where(last, 1, jnp.where(near, NEAR, max(n, NEAR)))
    own_latents(0)
    loop(early, ahead, encode)
    v_copy.wait()
    mlp_copy.wait()

    def step(i):
        live = i < n

        @pl.when(i + 1 < n)
        def _():
            own_latents(i + 1)

        @pl.when(i + ahead < n)
        def _():
            encode(i + ahead)

        @pl.when(live)
        def _():
            recon[span(i), :] = decoded(t, i)

        @pl.when(jnp.logical_and(live, t > 0))
        def _():
            relay(t - 1, i)

        j = i - grad_lag

        @pl.when(jnp.logical_and(j >= 0, j < n))
        def _():
            own_grad(j)

        @pl.when(live)
        def _():
            loop(2, t, lambda d: relay(t - d, i))

        @pl.when(jnp.logical_and(live, t > 1))
        def _():
            relay(0, i)

        @pl.when(live)
        def _():
            send_sums(i)

        j2 = i - back_lag

        @pl.when(jnp.logical_and(j2 >= 0, j2 < n))
        def _():
            backward(j2)

        @pl.when(jnp.logical_and(last, i == n + sum_lag))
        def _():
            loop(0, t + 1, dec_piece)

        j3 = i - sum_lag

        @pl.when(jnp.logical_and(below, jnp.logical_and(j3 >= 0, j3 < n)))
        def _():
            combine(j3)

        @pl.when(jnp.logical_and(j3 >= 1, j3 <= n))
        def _():
            masked(j3 - 1)

    loop(t + 1, layers, blank)
    loop(0, n + sum_lag + 1, step)

    def drain(j):
        for k in range(1, blocks):
            x_copy(j, k).wait_send()
            rs_copy(j, k).wait_send()
            og_copy(j, k).wait_send()
        lo_copy(j).wait_send()
        for h in range(2):
            hi_copy(j, h).wait_send()
            y_copy(j, h).wait_send()

        def passed(l):
            @pl.when(below)
            def _():
                for h in range(2):
                    zu_copy(l, j, h).wait_send()

            @pl.when(l < t)
            def _():
                for h in range(2):
                    zd_copy(l, j, h).wait_send()

        loop(0, t + 1, passed)

    loop(0, n, drain)


def exchange(layer_inputs, mlp_outputs, enc_weight, enc_bias, dec_weight):
    layers, latents, width = dec_weight.shape
    blocks = lax.axis_size("latent")
    rb, depth = layer_inputs.shape
    rows = rb * blocks
    half = latents // 2
    rscale = rows ** (-0.5)
    chunks = next((c for c in CHUNKS if rb % (16 * c) == 0), 1)
    hbm = pl.BlockSpec(memory_space=pltpu.HBM)
    dma = pltpu.SemaphoreType.DMA
    per_chunk = dma((chunks,))
    per_block = dma((chunks, blocks))
    per_layer = dma((layers, chunks, 2))
    per_side = dma((chunks, 2))
    sides = pltpu.VMEM((2, rows, half), BF16)
    sent = pltpu.VMEM((layers, 2, rows, half), BF16)
    return pl.pallas_call(
        functools.partial(exchange_kernel, layers, blocks, chunks, rscale),
        out_shape=(
            pltpu.VMEM((layers, latents, width), BF16),
            pltpu.VMEM((rows, depth), BF16),
            pltpu.VMEM((rows, latents), BF16),
        ),
        in_specs=[hbm] * 5,
        out_specs=(pl.BlockSpec(memory_space=pltpu.VMEM),) * 3,
        scratch_shapes=[
            pltpu.VMEM((rb, width), BF16),
            pltpu.VMEM((depth, latents), BF16),
            pltpu.VMEM((layers, latents), F32),
            pltpu.VMEM((layers, latents, width), BF16),
            pltpu.VMEM((2, rows, half), F32),
            sides, sides, sides, sides,
            sent,
            pltpu.VMEM((rows, width), F32),
            pltpu.VMEM((rows, width), BF16),
            pltpu.VMEM((blocks, rb, width), BF16),
            pltpu.VMEM((rows, width), BF16),
            pltpu.VMEM((layers, 2, rows, half), F32),
            sent, sent, sides, sides,
            per_block, per_block, per_side, per_side, per_chunk, per_chunk, per_layer, per_layer,
            per_block, per_block, per_block, per_block, per_layer, per_layer, per_side, per_side,
            per_chunk, dma((4,)),
        ],
        compiler_params=pltpu.CompilerParams(
            collective_id=0, has_side_effects=True, vmem_limit_bytes=40 * 2**20
        ),
        name="exchange",
    )(*(pltpu.with_memory_space_constraint(a, pltpu.HBM) for a in (layer_inputs, mlp_outputs, enc_weight, enc_bias, dec_weight)))


def finish_kernel(xg, pg, dec, enc_out, dec_out, enc, enc_sem, dec_sem):
    layers = dec.shape[0]
    piece = enc.shape[0] // layers
    writes = [pltpu.make_async_copy(dec.at[l], dec_out.at[l], dec_sem.at[l]) for l in range(layers)]
    for copy in writes:
        copy.start()
    for l in range(layers):
        part = pl.ds(l * piece, piece)
        enc[part, :] = lax.dot_general(
            xg[:, part], pg[...], (((0,), (0,)), ((), ())), preferred_element_type=F32
        )
        writes.append(pltpu.make_async_copy(enc.at[part], enc_out.at[part], enc_sem.at[l]))
        writes[-1].start()
    for copy in writes:
        copy.wait()


def local(layer_inputs, mlp_outputs, enc_weight, enc_bias, dec_weight):
    dec, xg, pg = exchange(layer_inputs, mlp_outputs, enc_weight, enc_bias, dec_weight)
    hbm = pl.BlockSpec(memory_space=pltpu.HBM)
    per_layer = pltpu.SemaphoreType.DMA((dec.shape[0],))
    return pl.pallas_call(
        finish_kernel,
        in_specs=[pl.BlockSpec(memory_space=pltpu.VMEM)] * 3,
        out_specs=(hbm,) * 2,
        out_shape=(
            jax.ShapeDtypeStruct(enc_weight.shape, F32),
            jax.ShapeDtypeStruct(dec_weight.shape, BF16),
        ),
        scratch_shapes=[pltpu.VMEM(enc_weight.shape, F32), per_layer, per_layer],
        compiler_params=pltpu.CompilerParams(vmem_limit_bytes=24 * 2**20),
        name="finish",
    )(xg, pg, dec)


def solution(mesh):
    in_specs = (
        P("latent", "layer"),
        P("latent", "layer"),
        P("layer", "latent"),
        P(None, "latent"),
        P(None, "latent", "layer"),
    )
    out_specs = (P("layer", "latent"), P(None, "latent", "layer"))
    return jax.shard_map(local, mesh=mesh, in_specs=in_specs, out_specs=out_specs, check_vma=False)
```

```python
import functools

import jax
import jax.numpy as jnp
from jax import lax
from jax.experimental import pallas as pl
from jax.experimental.pallas import tpu as pltpu
from jax.sharding import PartitionSpec as P

MESH = pl.DeviceIdType.MESH
F32 = jnp.float32
BF16 = jnp.bfloat16
CHUNKS = (6, 3, 2)
NEAR = 4
FROM = 1
SWAPS = 2


def exchange_kernel(
    layers, blocks, chunks, rscale,
    x_hbm, mlp_hbm, w_hbm, bias_hbm, v_hbm,
    dec, xg, pg,
    mlp, w, bias_all, v, pre, his, hir, los, lor, lat, recon, rss, rsr, og, acc, zds, zdr, ys, yr, bss, bsr,
    x_ss, x_rs, hi_ss, hi_rs, lo_ss, lo_rs, zu_ss, zu_rs, rs_ss, rs_rs, og_ss, og_rs, zd_ss, zd_rs, y_ss, y_rs,
    fs_ss, fs_rs, bs_ss, bs_rs, own_sem, in_sem,
):
    p = lax.axis_index("layer")
    q = lax.axis_index("latent")
    t = p // 2
    y = p % 2
    n = chunks
    top = layers - 1
    last = t == top
    below = t < top
    near = t == top - 1
    s = x_hbm.shape[0] // n
    size = s * blocks
    half = w.shape[1] // 2
    partner = (p + 1 - 2 * y, q)
    up = (p + 2, q)
    down = (p - 2, q)
    chips = blocks // 2
    other = 1 - y

    def blk(k):
        return ((q // 2 + k // 2) % chips) * 2 + (q % 2 + k % 2) % 2

    def span(j):
        return pl.ds(pl.multiple_of(j * size, size), size)

    def piece(j, b):
        return pl.ds(pl.multiple_of(j * size + b * s, s), s)

    def mine(j):
        return pl.ds(pl.multiple_of(j * s, s), s)

    def rcopy(src, dst, ss, rs, dev):
        return pltpu.make_async_remote_copy(
            src_ref=src, dst_ref=dst, send_sem=ss, recv_sem=rs, device_id=dev, device_id_type=MESH
        )

    def loop(lower, upper, step):
        def body(i, carry):
            step(i)
            return carry

        lax.fori_loop(lower, upper, body, 0)

    def settle(ref, sem):
        pltpu.make_async_copy(ref, ref, sem).wait()

    def own_x(j):
        return pltpu.make_async_copy(x_hbm.at[mine(j)], xg.at[piece(j, q)], own_sem)

    w_copy = pltpu.make_async_copy(w_hbm, w, in_sem.at[0])
    bias_copy = pltpu.make_async_copy(bias_hbm, bias_all, in_sem.at[1])
    mlp_copy = pltpu.make_async_copy(mlp_hbm, mlp, in_sem.at[2])
    v_copy = pltpu.make_async_copy(v_hbm, v, in_sem.at[3])
    for j in range(n):
        own_x(j).start()
    for copy in (w_copy, bias_copy, mlp_copy, v_copy):
        copy.start()

    barrier = pltpu.get_barrier_semaphore()
    for k in range(1, blocks):
        pl.semaphore_signal(barrier, inc=1, device_id=(p, blk(k)), device_id_type=MESH)
    pl.semaphore_signal(barrier, inc=1, device_id=partner, device_id_type=MESH)

    @pl.when(below)
    def _():
        pl.semaphore_signal(barrier, inc=1, device_id=up, device_id_type=MESH)

    @pl.when(t > 0)
    def _():
        pl.semaphore_signal(barrier, inc=1, device_id=down, device_id_type=MESH)

    neighbours = blocks + below.astype(jnp.int32) + (t > 0).astype(jnp.int32)
    pl.semaphore_wait(barrier, neighbours)

    others = list(range(2, blocks)) + [1]

    def x_copy(j, k):
        part = xg.at[piece(j, q)]
        return rcopy(part, part, x_ss, x_rs.at[j], (p, blk(k)))

    def send_x(j):
        for k in others:
            x_copy(j, k).start()

    arrivals = pl.ds(0, (blocks - 1) * s)
    departures = pl.ds(0, (blocks - 1) * s * n)
    settle(xg.at[pl.ds(0, s * n)], own_sem)
    loop(0, n, send_x)

    def part_of(h):
        return pl.ds(pl.multiple_of(h * half, half), half)

    def side(h):
        return slice(h * half, (h + 1) * half)

    def hi_copy(j, h):
        return rcopy(his.at[h, span(j)], hir.at[h, span(j)], hi_ss, hi_rs.at[j, h], partner)

    def lo_copy(j):
        return rcopy(los.at[:, span(j)], lor.at[:, span(j)], lo_ss, lo_rs.at[j], partner)

    def encode(j):
        settle(xg.at[arrivals], x_rs.at[j])
        for h in range(2):
            part = jnp.dot(xg[span(j), :], w[:, side(h)], preferred_element_type=F32)
            pre[h, span(j)] = part
            hi = part.astype(BF16)
            his[h, span(j)] = hi
            hi_copy(j, h).start()
            los[h, span(j)] = (part - hi.astype(F32)).astype(BF16)

    def zu_copy(l, j, h):
        part = lat.at[l, h, span(j)]
        return rcopy(part, part, zu_ss.at[l, h], zu_rs.at[l, j, h], up)

    bias_copy.wait()
    own_row = lax.broadcasted_iota(jnp.int32, bias_all.shape, 0) == t
    bias = jnp.sum(jnp.where(own_row, bias_all[...], 0.0), axis=0, keepdims=True)
    w_copy.wait()
    ahead = jnp.where(last, n, min(n, 3))
    early = min(n, 2)
    loop(0, early, encode)

    def decoded(l, j):
        return jnp.dot(lat[l, 0, span(j)], v[l, :half, :], preferred_element_type=F32) + jnp.dot(
            lat[l, 1, span(j)], v[l, half:, :], preferred_element_type=F32
        )

    def swapped(l, j):
        return jnp.logical_and(l == top - 1, jnp.logical_and(j >= FROM, j < FROM + SWAPS))

    def goes_up(l, j, h):
        return jnp.logical_and(below, jnp.logical_or(jnp.logical_not(swapped(l, j)), y == h))

    def own_latents(j):
        for h in range(2):
            hi_copy(j, h).wait_recv()
            total = pre[h, span(j)] + hir[h, span(j)].astype(F32) + bias[:, side(h)]
            pre[h, span(j)] = total
            lat[t, h, span(j)] = jnp.maximum(total, 0.0).astype(BF16)

            @pl.when(goes_up(t, j, h))
            def _():
                zu_copy(t, j, h).start()

        @pl.when(below)
        def _():
            lo_copy(j).start()

    def relay(l, j):
        for h in range(2):
            zu_copy(l, j, h).wait_recv()

            @pl.when(below)
            def _():
                zu_copy(l, j, h).start()

        recon[span(j), :] += decoded(l, j)

    def fs_copy(j, h):
        part = lat.at[top - 1, h, span(j)]
        return rcopy(part, part, fs_ss, fs_rs.at[j], partner)

    def add_half(j, h):
        recon[span(j), :] += jnp.dot(lat[top - 1, h, span(j)], v[top - 1, part_of(h), :], preferred_element_type=F32)

    def swap_half(j):
        zu_copy(top - 1, j, y).wait_recv()
        fs_copy(j, y).start()
        add_half(j, y)

    def relay_other(j):
        fs_copy(j, other).wait_recv()
        add_half(j, other)

    def rs_copy(j, k):
        b = blk(k)
        return rcopy(rss.at[piece(j, b)], rsr.at[q, mine(j)], rs_ss, rs_rs.at[j], (p, b))

    def send_sums(j):
        rss[span(j), :] = recon[span(j), :].astype(BF16)
        for k in others:
            rs_copy(j, k).start()

    def og_copy(j, k):
        part = og.at[piece(j, q)]
        return rcopy(part, part, og_ss, og_rs.at[j], (p, blk(k)))

    def own_grad(j):
        total = recon[piece(j, q), :]
        settle(rss.at[arrivals], rs_rs.at[j])
        for k in range(1, blocks):
            total = total + rsr[blk(k), mine(j)].astype(F32)
        og[piece(j, q), :] = ((total - mlp[mine(j), :].astype(F32)) * rscale).astype(BF16)
        for k in others:
            og_copy(j, k).start()

    def zd_copy(l, j, h):
        return rcopy(zds.at[l, h, span(j)], zdr.at[l, h, span(j)], zd_ss.at[l, h], zd_rs.at[l, j, h], down)

    def y_copy(j, h):
        return rcopy(ys.at[h, span(j)], yr.at[h, span(j)], y_ss, y_rs.at[j, h], partner)

    def bs_copy(j):
        return rcopy(bss.at[span(j)], bsr.at[span(j)], bs_ss, bs_rs.at[j], partner)

    def back(l, j, h):
        return lax.dot_general(
            og[span(j), :], v[l, part_of(h), :], (((1,), (1,)), ((), ())), preferred_element_type=F32
        )

    def send_down(l, j, h, total):
        zds[l, h, span(j)] = total.astype(BF16)
        zd_copy(l, j, h).start()

    def send_across(j, h, total):
        acc[t, h, span(j)] = total
        ys[h, span(j)] = total.astype(BF16)
        y_copy(j, h).start()

    def send_own(j):
        for h in range(2):
            ys[h, span(j)] = acc[top, h, span(j)].astype(BF16)
            y_copy(j, h).start()

    def backward(j):
        settle(og.at[arrivals], og_rs.at[j])

        @pl.when(last)
        def _():
            bss[span(j)] = back(top - 1, j, other).astype(BF16)
            bs_copy(j).start()

            @pl.when(j > 0)
            def _():
                send_own(j - 1)

            def produce(l):
                for h in range(2):
                    send_down(l, j, h, back(l, j, h))

            loop(0, top - 1, produce)
            for h in range(2):
                acc[top, h, span(j)] = back(top, j, h)
            acc[top - 1, y, span(j)] = back(top - 1, j, y)

            @pl.when(j == n - 1)
            def _():
                send_own(j)

        @pl.when(below)
        def _():
            def keep(l):
                for h in range(2):
                    acc[l, h, span(j)] = back(l, j, h)

            loop(0, t + 1, keep)

    def finish_swap(j):
        bs_copy(j).wait_recv()
        send_down(top - 1, j, y, acc[top - 1, y, span(j)] + bsr[span(j)].astype(F32))

    def summed(l, j, h):
        zd_copy(l, j, h).wait_recv()
        return acc[l, h, span(j)] + zdr[l, h, span(j)].astype(F32)

    def pass_on(j):
        def add(l):
            for h in range(2):
                send_down(l, j, h, summed(l, j, h))

            @pl.when(j == n - 1)
            def _():
                dec_piece(l)

        loop(0, t, add)

    def combine(j):
        @pl.when(near)
        def _():
            send_across(j, other, acc[t, other, span(j)])
            send_across(j, y, summed(t, j, y))

        @pl.when(jnp.logical_not(near))
        def _():
            for h in range(2):
                send_across(j, h, summed(t, j, h))

        @pl.when(j == n - 1)
        def _():
            dec_piece(t)

    def masked(j):
        lo_copy(j).wait_recv()
        for h in range(2):
            y_copy(j, h).wait_recv()
            active = pre[h, span(j)] + lor[h, span(j)].astype(F32) > 0.0
            total = acc[t, h, span(j)] + yr[h, span(j)].astype(F32)
            pg[span(j), side(h)] = jnp.where(active, total, 0.0).astype(BF16)

    def dec_piece(l):
        for h in range(2):
            part = lax.dot_general(lat[l, h], og[...], (((0,), (0,)), ((), ())), preferred_element_type=F32)
            dec[l, h * half:(h + 1) * half, :] = part.astype(BF16)

    def blank(l):
        dec[l] = jnp.zeros((2 * half, dec.shape[2]), BF16)

    grad_lag = jnp.where(last, 1, 2)
    back_lag = jnp.where(last, 1, 3)
    sum_lag = jnp.where(last, 1, jnp.where(near, NEAR, max(n, NEAR)))
    own_latents(0)
    loop(early, ahead, encode)
    v_copy.wait()
    mlp_copy.wait()

    def step(i):
        live = i < n
        j = i - grad_lag
        soon = jnp.logical_and(last, j == n - 1)

        @pl.when(jnp.logical_and(jnp.logical_and(j >= 0, j < n), jnp.logical_not(soon)))
        def _():
            own_grad(j)

        @pl.when(i + 1 < n)
        def _():
            own_latents(i + 1)

        @pl.when(i + ahead < n)
        def _():
            encode(i + ahead)

        @pl.when(live)
        def _():
            recon[span(i), :] = decoded(t, i)

        apart = jnp.logical_and(last, swapped(t - 1, i))

        @pl.when(jnp.logical_and(live, jnp.logical_and(t > 0, jnp.logical_not(apart))))
        def _():
            relay(t - 1, i)

        @pl.when(jnp.logical_and(live, apart))
        def _():
            swap_half(i)

        @pl.when(jnp.logical_and(last, jnp.logical_and(i >= 1, i < n + 1)))
        def _():
            lo_copy(i - 1).start()

        @pl.when(jnp.logical_and(last, jnp.logical_and(i >= 2, i < n)))
        def _():
            finish_swap(i - 2)

        @pl.when(live)
        def _():
            loop(2, t, lambda d: relay(t - d, i))

        j2 = i - back_lag
        first = jnp.logical_and(last, jnp.logical_and(j2 == 0, n > 1))

        @pl.when(first)
        def _():
            backward(j2)

        @pl.when(jnp.logical_and(live, t > 1))
        def _():
            relay(0, i)

        @pl.when(jnp.logical_and(live, apart))
        def _():
            relay_other(i)

        @pl.when(live)
        def _():
            send_sums(i)

        @pl.when(jnp.logical_and(last, i == n - 1))
        def _():
            own_grad(i)

        @pl.when(jnp.logical_and(jnp.logical_and(j2 >= 0, j2 < n), jnp.logical_not(first)))
        def _():
            backward(j2)

        @pl.when(jnp.logical_and(last, i == n))
        def _():
            loop(max(n - 2, 0), n, finish_swap)

        @pl.when(jnp.logical_and(last, i == n + sum_lag + 1))
        def _():
            loop(0, t + 1, dec_piece)

        j3 = i - sum_lag

        @pl.when(jnp.logical_and(below, jnp.logical_and(j3 >= 0, j3 < n)))
        def _():
            pass_on(j3)

        @pl.when(jnp.logical_and(below, jnp.logical_and(j3 >= 1, j3 <= n)))
        def _():
            combine(j3 - 1)

        @pl.when(jnp.logical_and(j3 >= 2, j3 <= n + 1))
        def _():
            masked(j3 - 2)

    loop(t + 1, layers, blank)
    loop(0, n + sum_lag + 2, step)

    for ref, sem in ((xg, x_ss), (rss, rs_ss), (og, og_ss)):
        settle(ref.at[departures], sem)
    for ref, sem in ((his, hi_ss), (los, lo_ss), (ys, y_ss)):
        settle(ref, sem)
    apart_rows = size * len(range(FROM, min(FROM + SWAPS, n)))

    @pl.when(last)
    def _():
        settle(bss, bs_ss)
        if apart_rows:
            settle(bss.at[pl.ds(0, apart_rows)], fs_ss)

    def drain(l):
        for h in range(2):
            less = jnp.logical_and(l == top - 1, y != h)

            @pl.when(jnp.logical_and(below, jnp.logical_not(less)))
            def _():
                settle(lat.at[l, h], zu_ss.at[l, h])

            @pl.when(jnp.logical_and(below, less))
            def _():
                settle(lat.at[l, h, pl.ds(0, size * n - apart_rows)], zu_ss.at[l, h])

            @pl.when(jnp.logical_and(l < t, jnp.logical_not(less)))
            def _():
                settle(zds.at[l, h], zd_ss.at[l, h])

    loop(0, t + 1, drain)


def exchange(layer_inputs, mlp_outputs, enc_weight, enc_bias, dec_weight):
    layers, latents, width = dec_weight.shape
    blocks = lax.axis_size("latent")
    rb, depth = layer_inputs.shape
    rows = rb * blocks
    half = latents // 2
    rscale = rows ** (-0.5)
    chunks = next((c for c in CHUNKS if rb % (16 * c) == 0), 1)
    hbm = pl.BlockSpec(memory_space=pltpu.HBM)
    dma = pltpu.SemaphoreType.DMA
    per_chunk = dma((chunks,))
    one = dma
    per_layer = dma((layers - 1, chunks, 2))
    sides_sent = dma((layers - 1, 2))
    per_side = dma((chunks, 2))
    sides = pltpu.VMEM((2, rows, half), BF16)
    sent = pltpu.VMEM((layers, 2, rows, half), BF16)
    return pl.pallas_call(
        functools.partial(exchange_kernel, layers, blocks, chunks, rscale),
        out_shape=(
            pltpu.VMEM((layers, latents, width), BF16),
            pltpu.VMEM((rows, depth), BF16),
            pltpu.VMEM((rows, latents), BF16),
        ),
        in_specs=[hbm] * 5,
        out_specs=(pl.BlockSpec(memory_space=pltpu.VMEM),) * 3,
        scratch_shapes=[
            pltpu.VMEM((rb, width), BF16),
            pltpu.VMEM((depth, latents), BF16),
            pltpu.VMEM((layers, latents), F32),
            pltpu.VMEM((layers, latents, width), BF16),
            pltpu.VMEM((2, rows, half), F32),
            sides, sides, sides, sides,
            sent,
            pltpu.VMEM((rows, width), F32),
            pltpu.VMEM((rows, width), BF16),
            pltpu.VMEM((blocks, rb, width), BF16),
            pltpu.VMEM((rows, width), BF16),
            pltpu.VMEM((layers, 2, rows, half), F32),
            sent, sent, sides, sides,
            pltpu.VMEM((rows, half), BF16), pltpu.VMEM((rows, half), BF16),
            one, per_chunk, one, per_side, one, per_chunk, sides_sent, per_layer,
            one, per_chunk, one, per_chunk, sides_sent, per_layer, one, per_side,
            one, per_chunk, one, per_chunk, one, dma((4,)),
        ],
        compiler_params=pltpu.CompilerParams(
            collective_id=0, has_side_effects=True, vmem_limit_bytes=40 * 2**20
        ),
        name="exchange",
    )(*(pltpu.with_memory_space_constraint(a, pltpu.HBM) for a in (layer_inputs, mlp_outputs, enc_weight, enc_bias, dec_weight)))


def finish_kernel(xg, pg, dec, enc_out, dec_out, enc, enc_sem, dec_sem):
    layers = dec.shape[0]
    piece = enc.shape[0] // layers
    writes = [pltpu.make_async_copy(dec.at[l], dec_out.at[l], dec_sem.at[l]) for l in range(layers)]
    for copy in writes:
        copy.start()
    for l in range(layers):
        part = pl.ds(l * piece, piece)
        enc[part, :] = lax.dot_general(
            xg[:, part], pg[...], (((0,), (0,)), ((), ())), preferred_element_type=F32
        )
        writes.append(pltpu.make_async_copy(enc.at[part], enc_out.at[part], enc_sem.at[l]))
        writes[-1].start()
    for copy in writes:
        copy.wait()


def local(layer_inputs, mlp_outputs, enc_weight, enc_bias, dec_weight):
    dec, xg, pg = exchange(layer_inputs, mlp_outputs, enc_weight, enc_bias, dec_weight)
    hbm = pl.BlockSpec(memory_space=pltpu.HBM)
    per_layer = pltpu.SemaphoreType.DMA((dec.shape[0],))
    return pl.pallas_call(
        finish_kernel,
        in_specs=[pl.BlockSpec(memory_space=pltpu.VMEM)] * 3,
        out_specs=(hbm,) * 2,
        out_shape=(
            jax.ShapeDtypeStruct(enc_weight.shape, F32),
            jax.ShapeDtypeStruct(dec_weight.shape, BF16),
        ),
        scratch_shapes=[pltpu.VMEM(enc_weight.shape, F32), per_layer, per_layer],
        compiler_params=pltpu.CompilerParams(vmem_limit_bytes=24 * 2**20),
        name="finish",
    )(xg, pg, dec)


def solution(mesh):
    in_specs = (
        P("latent", "layer"),
        P("latent", "layer"),
        P("layer", "latent"),
        P(None, "latent"),
        P(None, "latent", "layer"),
    )
    out_specs = (P("layer", "latent"), P(None, "latent", "layer"))
    return jax.shard_map(local, mesh=mesh, in_specs=in_specs, out_specs=out_specs, check_vma=False)
```

```python
import functools

import jax
import jax.numpy as jnp
from jax import lax
from jax.experimental import pallas as pl
from jax.experimental.pallas import tpu as pltpu
from jax.sharding import PartitionSpec as P

MESH = pl.DeviceIdType.MESH
F32 = jnp.float32
BF16 = jnp.bfloat16
CHUNKS = (6, 3, 2)
NEAR = 4
FROM = 1
SWAPS = 2


def exchange_kernel(
    layers, blocks, chunks, rscale,
    x_hbm, mlp_hbm, w_hbm, bias_hbm, v_hbm,
    dec, xg, pg,
    mlp, w, bias_all, v, pre, his, hir, los, lor, lat, recon, rss, rsr, og, acc, zds, zdr, ys, yr, bss, bsr, fas, far,
    x_ss, x_rs, hi_ss, hi_rs, lo_ss, lo_rs, zu_ss, zu_rs, rs_ss, rs_rs, og_ss, og_rs, zd_ss, zd_rs, y_ss, y_rs,
    fs_ss, fs_rs, bs_ss, bs_rs, fa_ss, fa_rs, own_sem, in_sem,
):
    p = lax.axis_index("layer")
    q = lax.axis_index("latent")
    t = p // 2
    y = p % 2
    n = chunks
    top = layers - 1
    last = t == top
    below = t < top
    near = t == top - 1
    s = x_hbm.shape[0] // n
    size = s * blocks
    half = w.shape[1] // 2
    partner = (p + 1 - 2 * y, q)
    up = (p + 2, q)
    down = (p - 2, q)
    chips = blocks // 2
    other = 1 - y

    def blk(k):
        return ((q // 2 + k // 2) % chips) * 2 + (q % 2 + k % 2) % 2

    def span(j):
        return pl.ds(pl.multiple_of(j * size, size), size)

    def piece(j, b):
        return pl.ds(pl.multiple_of(j * size + b * s, s), s)

    def mine(j):
        return pl.ds(pl.multiple_of(j * s, s), s)

    def rcopy(src, dst, ss, rs, dev):
        return pltpu.make_async_remote_copy(
            src_ref=src, dst_ref=dst, send_sem=ss, recv_sem=rs, device_id=dev, device_id_type=MESH
        )

    def loop(lower, upper, step):
        def body(i, carry):
            step(i)
            return carry

        lax.fori_loop(lower, upper, body, 0)

    def settle(ref, sem):
        pltpu.make_async_copy(ref, ref, sem).wait()

    def own_x(j):
        return pltpu.make_async_copy(x_hbm.at[mine(j)], xg.at[piece(j, q)], own_sem)

    w_copy = pltpu.make_async_copy(w_hbm, w, in_sem.at[0])
    bias_copy = pltpu.make_async_copy(bias_hbm, bias_all, in_sem.at[1])
    mlp_copy = pltpu.make_async_copy(mlp_hbm, mlp, in_sem.at[2])
    v_copy = pltpu.make_async_copy(v_hbm, v, in_sem.at[3])
    for j in range(n):
        own_x(j).start()
    for copy in (w_copy, bias_copy, mlp_copy, v_copy):
        copy.start()

    barrier = pltpu.get_barrier_semaphore()
    for k in range(1, blocks):
        pl.semaphore_signal(barrier, inc=1, device_id=(p, blk(k)), device_id_type=MESH)
    pl.semaphore_signal(barrier, inc=1, device_id=partner, device_id_type=MESH)

    @pl.when(below)
    def _():
        pl.semaphore_signal(barrier, inc=1, device_id=up, device_id_type=MESH)

    @pl.when(t > 0)
    def _():
        pl.semaphore_signal(barrier, inc=1, device_id=down, device_id_type=MESH)

    neighbours = blocks + below.astype(jnp.int32) + (t > 0).astype(jnp.int32)
    pl.semaphore_wait(barrier, neighbours)

    others = list(range(2, blocks)) + [1]

    def x_copy(j, k):
        part = xg.at[piece(j, q)]
        return rcopy(part, part, x_ss, x_rs.at[j], (p, blk(k)))

    def send_x(j):
        for k in others:
            x_copy(j, k).start()

    arrivals = pl.ds(0, (blocks - 1) * s)
    departures = pl.ds(0, (blocks - 1) * s * n)
    settle(xg.at[pl.ds(0, s * n)], own_sem)
    loop(0, n, send_x)

    def part_of(h):
        return pl.ds(pl.multiple_of(h * half, half), half)

    def side(h):
        return slice(h * half, (h + 1) * half)

    def hi_copy(j, h):
        return rcopy(his.at[h, span(j)], hir.at[h, span(j)], hi_ss, hi_rs.at[j, h], partner)

    def lo_copy(j):
        return rcopy(los.at[:, span(j)], lor.at[:, span(j)], lo_ss, lo_rs.at[j], partner)

    def encode(j):
        settle(xg.at[arrivals], x_rs.at[j])
        for h in range(2):
            part = jnp.dot(xg[span(j), :], w[:, side(h)], preferred_element_type=F32)
            pre[h, span(j)] = part
            hi = part.astype(BF16)
            his[h, span(j)] = hi
            hi_copy(j, h).start()
            los[h, span(j)] = (part - hi.astype(F32)).astype(BF16)

    def zu_copy(l, j, h):
        part = lat.at[l, h, span(j)]
        return rcopy(part, part, zu_ss.at[l, h], zu_rs.at[l, j, h], up)

    bias_copy.wait()
    own_row = lax.broadcasted_iota(jnp.int32, bias_all.shape, 0) == t
    bias = jnp.sum(jnp.where(own_row, bias_all[...], 0.0), axis=0, keepdims=True)
    w_copy.wait()
    ahead = jnp.where(last, n, min(n, 3))
    early = min(n, 2)
    loop(0, early, encode)

    def decoded(l, j):
        return jnp.dot(lat[l, 0, span(j)], v[l, :half, :], preferred_element_type=F32) + jnp.dot(
            lat[l, 1, span(j)], v[l, half:, :], preferred_element_type=F32
        )

    def swapped(l, j):
        return jnp.logical_and(l == top - 1, jnp.logical_and(j >= FROM, j < FROM + SWAPS))

    def goes_up(l, j, h):
        return jnp.logical_and(below, jnp.logical_or(jnp.logical_not(swapped(l, j)), y == h))

    def own_latents(j):
        for h in range(2):
            hi_copy(j, h).wait_recv()
            total = pre[h, span(j)] + hir[h, span(j)].astype(F32) + bias[:, side(h)]
            pre[h, span(j)] = total
            lat[t, h, span(j)] = jnp.maximum(total, 0.0).astype(BF16)

            @pl.when(goes_up(t, j, h))
            def _():
                zu_copy(t, j, h).start()

        @pl.when(below)
        def _():
            lo_copy(j).start()

    def relay(l, j):
        for h in range(2):
            zu_copy(l, j, h).wait_recv()

            @pl.when(below)
            def _():
                zu_copy(l, j, h).start()

        recon[span(j), :] += decoded(l, j)

    def fs_copy(j, h):
        part = lat.at[top - 1, h, span(j)]
        return rcopy(part, part, fs_ss, fs_rs.at[j], partner)

    def add_half(j, h):
        recon[span(j), :] += jnp.dot(lat[top - 1, h, span(j)], v[top - 1, part_of(h), :], preferred_element_type=F32)

    def swap_half(j):
        zu_copy(top - 1, j, y).wait_recv()
        fs_copy(j, y).start()
        add_half(j, y)

    def relay_other(j):
        fs_copy(j, other).wait_recv()
        add_half(j, other)

    def rs_copy(j, k):
        b = blk(k)
        return rcopy(rss.at[piece(j, b)], rsr.at[q, mine(j)], rs_ss, rs_rs.at[j], (p, b))

    def send_sums(j):
        rss[span(j), :] = recon[span(j), :].astype(BF16)
        for k in others:
            rs_copy(j, k).start()

    def og_copy(j, k):
        part = og.at[piece(j, q)]
        return rcopy(part, part, og_ss, og_rs.at[j], (p, blk(k)))

    def own_grad(j):
        total = recon[piece(j, q), :]
        settle(rss.at[arrivals], rs_rs.at[j])
        for k in range(1, blocks):
            total = total + rsr[blk(k), mine(j)].astype(F32)
        og[piece(j, q), :] = ((total - mlp[mine(j), :].astype(F32)) * rscale).astype(BF16)
        for k in others:
            og_copy(j, k).start()

    def zd_copy(l, j, h):
        return rcopy(zds.at[l, h, span(j)], zdr.at[l, h, span(j)], zd_ss.at[l, h], zd_rs.at[l, j, h], down)

    def y_copy(j, h):
        return rcopy(ys.at[h, span(j)], yr.at[h, span(j)], y_ss, y_rs.at[j, h], partner)

    def bs_copy(j):
        return rcopy(bss.at[span(j)], bsr.at[span(j)], bs_ss, bs_rs.at[j], partner)

    def back(l, j, h):
        return lax.dot_general(
            og[span(j), :], v[l, part_of(h), :], (((1,), (1,)), ((), ())), preferred_element_type=F32
        )

    def send_down(l, j, h, total):
        zds[l, h, span(j)] = total.astype(BF16)
        zd_copy(l, j, h).start()

    def far_copy(l, h):
        return rcopy(fas.at[l, h], far.at[t, h], fa_ss.at[l], fa_rs.at[t, h], (p - 2 * (t - l), q))

    def far_in(u, h):
        return rcopy(fas.at[t, h], far.at[u, h], fa_ss.at[t], fa_rs.at[u, h], (p + 2 * (u - t), q))

    def send_far(l, h, total):
        fas[l, h] = total.astype(BF16)
        far_copy(l, h).start()

    def send_across(j, h, total):
        acc[t, h, span(j)] = total
        ys[h, span(j)] = total.astype(BF16)
        y_copy(j, h).start()

    def send_own(j):
        for h in range(2):
            ys[h, span(j)] = acc[top, h, span(j)].astype(BF16)
            y_copy(j, h).start()

    def backward(j):
        settle(og.at[arrivals], og_rs.at[j])

        @pl.when(last)
        def _():
            def produce(l):
                for h in range(2):
                    send_down(l, j, h, back(l, j, h))

            loop(0, min(top - 1, 1), produce)
            bss[span(j)] = back(top - 1, j, other).astype(BF16)
            bs_copy(j).start()

            @pl.when(j > 0)
            def _():
                send_own(j - 1)

            loop(min(top - 1, 1), top - 1, produce)
            for h in range(2):
                acc[top, h, span(j)] = back(top, j, h)
            acc[top - 1, y, span(j)] = back(top - 1, j, y)

            @pl.when(j == n - 1)
            def _():
                send_own(j)

        @pl.when(below)
        def _():
            def keep(l):
                for h in range(2):
                    total = back(l, j, h)
                    alone = jnp.logical_and(jnp.logical_and(j == n - 1, l < t), jnp.logical_not(near))

                    @pl.when(alone)
                    def _():
                        send_far(l, h, total)

                    @pl.when(jnp.logical_not(alone))
                    def _():
                        acc[l, h, span(j)] = total

            loop(0, t + 1, keep)

            @pl.when(near)
            def _():
                send_across(j, other, acc[t, other, span(j)])

    def finish_swap(j):
        bs_copy(j).wait_recv()
        send_down(top - 1, j, y, acc[top - 1, y, span(j)] + bsr[span(j)].astype(F32))

    def summed(l, j, h):
        zd_copy(l, j, h).wait_recv()
        return acc[l, h, span(j)] + zdr[l, h, span(j)].astype(F32)

    def pass_on(j):
        final = j == n - 1

        def add(l):
            for h in range(2):
                @pl.when(jnp.logical_not(final))
                def _():
                    send_down(l, j, h, summed(l, j, h))

                @pl.when(jnp.logical_and(final, near))
                def _():
                    send_far(l, h, summed(l, j, h))

            @pl.when(final)
            def _():
                dec_piece(l)

        loop(0, t, add)

    def combine(j):
        final = j == n - 1

        @pl.when(near)
        def _():
            send_across(j, y, summed(t, j, y))

        @pl.when(jnp.logical_not(jnp.logical_or(near, final)))
        def _():
            for h in range(2):
                send_across(j, h, summed(t, j, h))

        @pl.when(jnp.logical_and(final, jnp.logical_not(near)))
        def _():
            for h in range(2):
                def add_far(u):
                    far_in(u, h).wait_recv()
                    acc[t, h, span(j)] += far[u, h].astype(F32)

                loop(t + 1, top, add_far)
                send_across(j, h, acc[t, h, span(j)])

        @pl.when(final)
        def _():
            dec_piece(t)

    def masked(j):
        lo_copy(j).wait_recv()
        for h in range(2):
            y_copy(j, h).wait_recv()
            active = pre[h, span(j)] + lor[h, span(j)].astype(F32) > 0.0
            total = acc[t, h, span(j)] + yr[h, span(j)].astype(F32)
            pg[span(j), side(h)] = jnp.where(active, total, 0.0).astype(BF16)

    def dec_piece(l):
        for h in range(2):
            part = lax.dot_general(lat[l, h], og[...], (((0,), (0,)), ((), ())), preferred_element_type=F32)
            dec[l, h * half:(h + 1) * half, :] = part.astype(BF16)

    def blank(l):
        dec[l] = jnp.zeros((2 * half, dec.shape[2]), BF16)

    grad_lag = jnp.where(last, 1, 2)
    back_lag = jnp.where(last, 1, 3)
    sum_lag = jnp.where(last, 1, jnp.where(near, NEAR, max(n, NEAR)))
    own_latents(0)
    loop(early, ahead, encode)
    v_copy.wait()
    mlp_copy.wait()

    def step(i):
        live = i < n
        j = i - grad_lag
        soon = jnp.logical_and(last, j == n - 1)

        @pl.when(jnp.logical_and(jnp.logical_and(j >= 0, j < n), jnp.logical_not(soon)))
        def _():
            own_grad(j)

        @pl.when(i + 1 < n)
        def _():
            own_latents(i + 1)

        @pl.when(i + ahead < n)
        def _():
            encode(i + ahead)

        @pl.when(live)
        def _():
            recon[span(i), :] = decoded(t, i)

        apart = jnp.logical_and(last, swapped(t - 1, i))

        @pl.when(jnp.logical_and(live, jnp.logical_and(t > 0, jnp.logical_not(apart))))
        def _():
            relay(t - 1, i)

        @pl.when(jnp.logical_and(live, apart))
        def _():
            swap_half(i)

        @pl.when(jnp.logical_and(last, jnp.logical_and(i >= 1, i < n + 1)))
        def _():
            lo_copy(i - 1).start()

        @pl.when(jnp.logical_and(last, jnp.logical_and(i >= 2, i < n)))
        def _():
            finish_swap(i - 2)

        @pl.when(live)
        def _():
            loop(2, t, lambda d: relay(t - d, i))

        j2 = i - back_lag
        first = jnp.logical_and(last, jnp.logical_and(j2 == 0, n > 1))

        @pl.when(first)
        def _():
            backward(j2)

        @pl.when(jnp.logical_and(live, t > 1))
        def _():
            relay(0, i)

        @pl.when(jnp.logical_and(live, apart))
        def _():
            relay_other(i)

        @pl.when(live)
        def _():
            send_sums(i)

        @pl.when(jnp.logical_and(last, i == n - 1))
        def _():
            own_grad(i)

        @pl.when(jnp.logical_and(jnp.logical_and(j2 >= 0, j2 < n), jnp.logical_not(first)))
        def _():
            backward(j2)

        @pl.when(jnp.logical_and(last, i == n))
        def _():
            loop(max(n - 2, 0), n, finish_swap)

        @pl.when(jnp.logical_and(last, i == n + sum_lag + 1))
        def _():
            loop(0, t + 1, dec_piece)

        j3 = i - sum_lag

        @pl.when(jnp.logical_and(below, jnp.logical_and(j3 >= 0, j3 < n)))
        def _():
            pass_on(j3)

        @pl.when(jnp.logical_and(below, jnp.logical_and(j3 >= 1, j3 <= n)))
        def _():
            combine(j3 - 1)

        @pl.when(jnp.logical_and(j3 >= 2, j3 <= n + 1))
        def _():
            masked(j3 - 2)

    loop(t + 1, layers, blank)
    loop(0, n + sum_lag + 2, step)

    for ref, sem in ((xg, x_ss), (rss, rs_ss), (og, og_ss)):
        settle(ref.at[departures], sem)
    for ref, sem in ((his, hi_ss), (los, lo_ss), (ys, y_ss)):
        settle(ref, sem)
    apart_rows = size * len(range(FROM, min(FROM + SWAPS, n)))

    @pl.when(last)
    def _():
        settle(bss, bs_ss)
        if apart_rows:
            settle(bss.at[pl.ds(0, apart_rows)], fs_ss)

    def drain(l):
        for h in range(2):
            less = jnp.logical_and(l == top - 1, y != h)

            @pl.when(jnp.logical_and(below, jnp.logical_not(less)))
            def _():
                settle(lat.at[l, h], zu_ss.at[l, h])

            @pl.when(jnp.logical_and(below, less))
            def _():
                settle(lat.at[l, h, pl.ds(0, size * n - apart_rows)], zu_ss.at[l, h])

            @pl.when(jnp.logical_and(last, jnp.logical_and(l < t, jnp.logical_not(less))))
            def _():
                settle(zds.at[l, h], zd_ss.at[l, h])

            if n > 1:
                @pl.when(jnp.logical_and(below, l < t))
                def _():
                    settle(zds.at[l, h, pl.ds(0, size * (n - 1))], zd_ss.at[l, h])

        @pl.when(jnp.logical_and(below, l < t))
        def _():
            settle(fas.at[l], fa_ss.at[l])

    loop(0, t + 1, drain)


def exchange(layer_inputs, mlp_outputs, enc_weight, enc_bias, dec_weight):
    layers, latents, width = dec_weight.shape
    blocks = lax.axis_size("latent")
    rb, depth = layer_inputs.shape
    rows = rb * blocks
    half = latents // 2
    rscale = rows ** (-0.5)
    chunks = next((c for c in CHUNKS if rb % (16 * c) == 0), 1)
    hbm = pl.BlockSpec(memory_space=pltpu.HBM)
    dma = pltpu.SemaphoreType.DMA
    per_chunk = dma((chunks,))
    one = dma
    per_layer = dma((layers - 1, chunks, 2))
    sides_sent = dma((layers - 1, 2))
    per_side = dma((chunks, 2))
    sides = pltpu.VMEM((2, rows, half), BF16)
    sent = pltpu.VMEM((layers, 2, rows, half), BF16)
    one_chunk = pltpu.VMEM((layers, 2, rows // chunks, half), BF16)
    return pl.pallas_call(
        functools.partial(exchange_kernel, layers, blocks, chunks, rscale),
        out_shape=(
            pltpu.VMEM((layers, latents, width), BF16),
            pltpu.VMEM((rows, depth), BF16),
            pltpu.VMEM((rows, latents), BF16),
        ),
        in_specs=[hbm] * 5,
        out_specs=(pl.BlockSpec(memory_space=pltpu.VMEM),) * 3,
        scratch_shapes=[
            pltpu.VMEM((rb, width), BF16),
            pltpu.VMEM((depth, latents), BF16),
            pltpu.VMEM((layers, latents), F32),
            pltpu.VMEM((layers, latents, width), BF16),
            pltpu.VMEM((2, rows, half), F32),
            sides, sides, sides, sides,
            sent,
            pltpu.VMEM((rows, width), F32),
            pltpu.VMEM((rows, width), BF16),
            pltpu.VMEM((blocks, rb, width), BF16),
            pltpu.VMEM((rows, width), BF16),
            pltpu.VMEM((layers, 2, rows, half), F32),
            sent, sent, sides, sides,
            pltpu.VMEM((rows, half), BF16), pltpu.VMEM((rows, half), BF16), one_chunk, one_chunk,
            one, per_chunk, one, per_side, one, per_chunk, sides_sent, per_layer,
            one, per_chunk, one, per_chunk, sides_sent, per_layer, one, per_side,
            one, per_chunk, one, per_chunk, dma((layers,)), dma((layers, 2)), one, dma((4,)),
        ],
        compiler_params=pltpu.CompilerParams(
            collective_id=0, has_side_effects=True, vmem_limit_bytes=40 * 2**20
        ),
        name="exchange",
    )(*(pltpu.with_memory_space_constraint(a, pltpu.HBM) for a in (layer_inputs, mlp_outputs, enc_weight, enc_bias, dec_weight)))


def finish_kernel(xg, pg, dec, enc_out, dec_out, enc, enc_sem, dec_sem):
    layers = dec.shape[0]
    piece = enc.shape[0] // layers
    writes = [pltpu.make_async_copy(dec.at[l], dec_out.at[l], dec_sem.at[l]) for l in range(layers)]
    for copy in writes:
        copy.start()
    for l in range(layers):
        part = pl.ds(l * piece, piece)
        enc[part, :] = lax.dot_general(
            xg[:, part], pg[...], (((0,), (0,)), ((), ())), preferred_element_type=F32
        )
        writes.append(pltpu.make_async_copy(enc.at[part], enc_out.at[part], enc_sem.at[l]))
        writes[-1].start()
    for copy in writes:
        copy.wait()


def local(layer_inputs, mlp_outputs, enc_weight, enc_bias, dec_weight):
    dec, xg, pg = exchange(layer_inputs, mlp_outputs, enc_weight, enc_bias, dec_weight)
    hbm = pl.BlockSpec(memory_space=pltpu.HBM)
    per_layer = pltpu.SemaphoreType.DMA((dec.shape[0],))
    return pl.pallas_call(
        finish_kernel,
        in_specs=[pl.BlockSpec(memory_space=pltpu.VMEM)] * 3,
        out_specs=(hbm,) * 2,
        out_shape=(
            jax.ShapeDtypeStruct(enc_weight.shape, F32),
            jax.ShapeDtypeStruct(dec_weight.shape, BF16),
        ),
        scratch_shapes=[pltpu.VMEM(enc_weight.shape, F32), per_layer, per_layer],
        compiler_params=pltpu.CompilerParams(vmem_limit_bytes=24 * 2**20),
        name="finish",
    )(xg, pg, dec)


def solution(mesh):
    in_specs = (
        P("latent", "layer"),
        P("latent", "layer"),
        P("layer", "latent"),
        P(None, "latent"),
        P(None, "latent", "layer"),
    )
    out_specs = (P("layer", "latent"), P(None, "latent", "layer"))
    return jax.shard_map(local, mesh=mesh, in_specs=in_specs, out_specs=out_specs, check_vma=False)
```

```python
import functools

import jax
import jax.numpy as jnp
from jax import lax
from jax.experimental import pallas as pl
from jax.experimental.pallas import tpu as pltpu
from jax.sharding import PartitionSpec as P

MESH = pl.DeviceIdType.MESH
F32 = jnp.float32
BF16 = jnp.bfloat16
CHUNKS = (6, 3, 2)
NEAR = 4
FROM = 2
SWAPS = 2


def exchange_kernel(
    layers, blocks, chunks, rscale,
    x_hbm, mlp_hbm, w_hbm, bias_hbm, v_hbm,
    dec, xg, pg,
    mlp, w, bias_all, v, pre, his, hir, los, lor, lat, recon, rss, rsr, og, acc, zds, zdr, ys, yr, bss, bsr, fas, far,
    x_ss, x_rs, hi_ss, hi_rs, lo_ss, lo_rs, zu_ss, zu_rs, rs_ss, rs_rs, og_ss, og_rs, zd_ss, zd_rs, y_ss, y_rs,
    fs_ss, fs_rs, bs_ss, bs_rs, fa_ss, fa_rs, own_sem, in_sem,
):
    p = lax.axis_index("layer")
    q = lax.axis_index("latent")
    t = p // 2
    y = p % 2
    n = chunks
    top = layers - 1
    last = t == top
    below = t < top
    near = t == top - 1
    s = x_hbm.shape[0] // n
    size = s * blocks
    half = w.shape[1] // 2
    partner = (p + 1 - 2 * y, q)
    up = (p + 2, q)
    down = (p - 2, q)
    chips = blocks // 2
    other = 1 - y

    def blk(k):
        return ((q // 2 + k // 2) % chips) * 2 + (q % 2 + k % 2) % 2

    def span(j):
        return pl.ds(pl.multiple_of(j * size, size), size)

    def piece(j, b):
        return pl.ds(pl.multiple_of(j * size + b * s, s), s)

    def mine(j):
        return pl.ds(pl.multiple_of(j * s, s), s)

    def rcopy(src, dst, ss, rs, dev):
        return pltpu.make_async_remote_copy(
            src_ref=src, dst_ref=dst, send_sem=ss, recv_sem=rs, device_id=dev, device_id_type=MESH
        )

    def loop(lower, upper, step):
        def body(i, carry):
            step(i)
            return carry

        lax.fori_loop(lower, upper, body, 0)

    def settle(ref, sem):
        pltpu.make_async_copy(ref, ref, sem).wait()

    def own_x(j):
        return pltpu.make_async_copy(x_hbm.at[mine(j)], xg.at[piece(j, q)], own_sem)

    w_copy = pltpu.make_async_copy(w_hbm, w, in_sem.at[0])
    bias_copy = pltpu.make_async_copy(bias_hbm, bias_all, in_sem.at[1])
    mlp_copy = pltpu.make_async_copy(mlp_hbm, mlp, in_sem.at[2])
    v_copy = pltpu.make_async_copy(v_hbm, v, in_sem.at[3])
    for j in range(n):
        own_x(j).start()
    for copy in (w_copy, bias_copy, mlp_copy, v_copy):
        copy.start()

    barrier = pltpu.get_barrier_semaphore()
    for k in range(1, blocks):
        pl.semaphore_signal(barrier, inc=1, device_id=(p, blk(k)), device_id_type=MESH)
    pl.semaphore_signal(barrier, inc=1, device_id=partner, device_id_type=MESH)

    @pl.when(below)
    def _():
        pl.semaphore_signal(barrier, inc=1, device_id=up, device_id_type=MESH)

    @pl.when(t > 0)
    def _():
        pl.semaphore_signal(barrier, inc=1, device_id=down, device_id_type=MESH)

    neighbours = blocks + below.astype(jnp.int32) + (t > 0).astype(jnp.int32)
    pl.semaphore_wait(barrier, neighbours)

    others = list(range(2, blocks)) + [1]

    def x_copy(j, k):
        part = xg.at[piece(j, q)]
        return rcopy(part, part, x_ss, x_rs.at[j], (p, blk(k)))

    def send_x(j):
        for k in others:
            x_copy(j, k).start()

    arrivals = pl.ds(0, (blocks - 1) * s)
    departures = pl.ds(0, (blocks - 1) * s * n)
    settle(xg.at[pl.ds(0, s * n)], own_sem)
    loop(0, n, send_x)

    def part_of(h):
        return pl.ds(pl.multiple_of(h * half, half), half)

    def side(h):
        return slice(h * half, (h + 1) * half)

    def hi_copy(j, h):
        return rcopy(his.at[h, span(j)], hir.at[h, span(j)], hi_ss, hi_rs.at[j, h], partner)

    def lo_copy(j):
        return rcopy(los.at[:, span(j)], lor.at[:, span(j)], lo_ss, lo_rs.at[j], partner)

    def encode(j):
        settle(xg.at[arrivals], x_rs.at[j])
        for h in range(2):
            part = jnp.dot(xg[span(j), :], w[:, side(h)], preferred_element_type=F32)
            pre[h, span(j)] = part
            hi = part.astype(BF16)
            his[h, span(j)] = hi
            hi_copy(j, h).start()
            los[h, span(j)] = (part - hi.astype(F32)).astype(BF16)

    def zu_copy(l, j, h):
        part = lat.at[l, h, span(j)]
        return rcopy(part, part, zu_ss.at[l, h], zu_rs.at[l, j, h], up)

    bias_copy.wait()
    own_row = lax.broadcasted_iota(jnp.int32, bias_all.shape, 0) == t
    bias = jnp.sum(jnp.where(own_row, bias_all[...], 0.0), axis=0, keepdims=True)
    w_copy.wait()
    ahead = jnp.where(last, n, min(n, 3))
    early = min(n, 2)
    loop(0, early, encode)

    def decoded(l, j):
        return jnp.dot(lat[l, 0, span(j)], v[l, :half, :], preferred_element_type=F32) + jnp.dot(
            lat[l, 1, span(j)], v[l, half:, :], preferred_element_type=F32
        )

    def swapped(l, j):
        return jnp.logical_and(l == top - 1, jnp.logical_and(j >= FROM, j < FROM + SWAPS))

    def goes_up(l, j, h):
        return jnp.logical_and(below, jnp.logical_or(jnp.logical_not(swapped(l, j)), y == h))

    def own_latents(j):
        for h in range(2):
            hi_copy(j, h).wait_recv()
            total = pre[h, span(j)] + hir[h, span(j)].astype(F32) + bias[:, side(h)]
            pre[h, span(j)] = total
            lat[t, h, span(j)] = jnp.maximum(total, 0.0).astype(BF16)

            @pl.when(goes_up(t, j, h))
            def _():
                zu_copy(t, j, h).start()

        @pl.when(below)
        def _():
            lo_copy(j).start()

    def relay(l, j):
        for h in range(2):
            zu_copy(l, j, h).wait_recv()

            @pl.when(below)
            def _():
                zu_copy(l, j, h).start()

        recon[span(j), :] += decoded(l, j)

    def fs_copy(j, h):
        part = lat.at[top - 1, h, span(j)]
        return rcopy(part, part, fs_ss, fs_rs.at[j], partner)

    def add_half(j, h):
        recon[span(j), :] += jnp.dot(lat[top - 1, h, span(j)], v[top - 1, part_of(h), :], preferred_element_type=F32)

    def swap_half(j):
        zu_copy(top - 1, j, y).wait_recv()
        fs_copy(j, y).start()
        add_half(j, y)

    def relay_other(j):
        fs_copy(j, other).wait_recv()
        add_half(j, other)

    def rs_copy(j, k):
        b = blk(k)
        return rcopy(rss.at[piece(j, b)], rsr.at[q, mine(j)], rs_ss, rs_rs.at[j], (p, b))

    def send_sums(j):
        rss[span(j), :] = recon[span(j), :].astype(BF16)
        for k in others:
            rs_copy(j, k).start()

    def og_copy(j, k):
        part = og.at[piece(j, q)]
        return rcopy(part, part, og_ss, og_rs.at[j], (p, blk(k)))

    def own_grad(j):
        total = recon[piece(j, q), :]
        settle(rss.at[arrivals], rs_rs.at[j])
        for k in range(1, blocks):
            total = total + rsr[blk(k), mine(j)].astype(F32)
        og[piece(j, q), :] = ((total - mlp[mine(j), :].astype(F32)) * rscale).astype(BF16)
        for k in others:
            og_copy(j, k).start()

    def zd_copy(l, j, h):
        return rcopy(zds.at[l, h, span(j)], zdr.at[l, h, span(j)], zd_ss.at[l, h], zd_rs.at[l, j, h], down)

    def y_copy(j, h):
        return rcopy(ys.at[h, span(j)], yr.at[h, span(j)], y_ss, y_rs.at[j, h], partner)

    def bs_copy(j):
        return rcopy(bss.at[span(j)], bsr.at[span(j)], bs_ss, bs_rs.at[j], partner)

    def back(l, j, h):
        return lax.dot_general(
            og[span(j), :], v[l, part_of(h), :], (((1,), (1,)), ((), ())), preferred_element_type=F32
        )

    def send_down(l, j, h, total):
        zds[l, h, span(j)] = total.astype(BF16)
        zd_copy(l, j, h).start()

    def far_copy(l, h):
        return rcopy(fas.at[l, h], far.at[t, h], fa_ss.at[l], fa_rs.at[t, h], (p - 2 * (t - l), q))

    def far_in(u, h):
        return rcopy(fas.at[t, h], far.at[u, h], fa_ss.at[t], fa_rs.at[u, h], (p + 2 * (u - t), q))

    def send_far(l, h, total):
        fas[l, h] = total.astype(BF16)
        far_copy(l, h).start()

    def send_across(j, h, total):
        acc[t, h, span(j)] = total
        ys[h, span(j)] = total.astype(BF16)
        y_copy(j, h).start()

    def send_own(j):
        for h in range(2):
            ys[h, span(j)] = acc[top, h, span(j)].astype(BF16)
            y_copy(j, h).start()

    def backward(j):
        settle(og.at[arrivals], og_rs.at[j])

        @pl.when(last)
        def _():
            def produce(l):
                for h in range(2):
                    send_down(l, j, h, back(l, j, h))

            loop(0, min(top - 1, 1), produce)
            bss[span(j)] = back(top - 1, j, other).astype(BF16)
            bs_copy(j).start()

            @pl.when(j > 0)
            def _():
                send_own(j - 1)

            loop(min(top - 1, 1), top - 1, produce)
            for h in range(2):
                acc[top, h, span(j)] = back(top, j, h)
            acc[top - 1, y, span(j)] = back(top - 1, j, y)

            @pl.when(j == n - 1)
            def _():
                send_own(j)

        @pl.when(below)
        def _():
            def keep(l):
                for h in range(2):
                    total = back(l, j, h)
                    alone = jnp.logical_and(jnp.logical_and(j == n - 1, l < t), jnp.logical_not(near))

                    @pl.when(alone)
                    def _():
                        send_far(l, h, total)

                    @pl.when(jnp.logical_not(alone))
                    def _():
                        acc[l, h, span(j)] = total

            loop(0, t + 1, keep)

            @pl.when(near)
            def _():
                send_across(j, other, acc[t, other, span(j)])

    def finish_swap(j):
        bs_copy(j).wait_recv()
        send_down(top - 1, j, y, acc[top - 1, y, span(j)] + bsr[span(j)].astype(F32))

    def summed(l, j, h):
        zd_copy(l, j, h).wait_recv()
        return acc[l, h, span(j)] + zdr[l, h, span(j)].astype(F32)

    def pass_on(j):
        final = j == n - 1

        def add(l):
            for h in range(2):
                @pl.when(jnp.logical_not(final))
                def _():
                    send_down(l, j, h, summed(l, j, h))

                @pl.when(jnp.logical_and(final, near))
                def _():
                    send_far(l, h, summed(l, j, h))

            @pl.when(final)
            def _():
                dec_piece(l)

        loop(0, t, add)

    def combine(j):
        final = j == n - 1

        @pl.when(near)
        def _():
            send_across(j, y, summed(t, j, y))

        @pl.when(jnp.logical_not(jnp.logical_or(near, final)))
        def _():
            for h in range(2):
                send_across(j, h, summed(t, j, h))

        @pl.when(jnp.logical_and(final, jnp.logical_not(near)))
        def _():
            for h in range(2):
                def add_far(u):
                    far_in(u, h).wait_recv()
                    acc[t, h, span(j)] += far[u, h].astype(F32)

                loop(t + 1, top, add_far)
                send_across(j, h, acc[t, h, span(j)])

        @pl.when(final)
        def _():
            dec_piece(t)

    def masked(j):
        lo_copy(j).wait_recv()
        for h in range(2):
            y_copy(j, h).wait_recv()
            active = pre[h, span(j)] + lor[h, span(j)].astype(F32) > 0.0
            total = acc[t, h, span(j)] + yr[h, span(j)].astype(F32)
            pg[span(j), side(h)] = jnp.where(active, total, 0.0).astype(BF16)

    def dec_piece(l):
        for h in range(2):
            part = lax.dot_general(lat[l, h], og[...], (((0,), (0,)), ((), ())), preferred_element_type=F32)
            dec[l, h * half:(h + 1) * half, :] = part.astype(BF16)

    def blank(l):
        dec[l] = jnp.zeros((2 * half, dec.shape[2]), BF16)

    grad_lag = jnp.where(last, 1, 2)
    back_lag = jnp.where(last, 1, 3)
    sum_lag = jnp.where(last, 1, jnp.where(near, NEAR, max(n, NEAR)))
    own_latents(0)
    loop(early, ahead, encode)
    v_copy.wait()
    mlp_copy.wait()

    def step(i):
        live = i < n
        j = i - grad_lag
        soon = jnp.logical_and(last, j == n - 1)

        @pl.when(jnp.logical_and(jnp.logical_and(j >= 0, j < n), jnp.logical_not(soon)))
        def _():
            own_grad(j)

        @pl.when(i + 1 < n)
        def _():
            own_latents(i + 1)

        @pl.when(i + ahead < n)
        def _():
            encode(i + ahead)

        @pl.when(live)
        def _():
            recon[span(i), :] = decoded(t, i)

        apart = jnp.logical_and(last, swapped(t - 1, i))

        @pl.when(jnp.logical_and(live, jnp.logical_and(t > 0, jnp.logical_not(apart))))
        def _():
            relay(t - 1, i)

        @pl.when(jnp.logical_and(live, apart))
        def _():
            swap_half(i)

        @pl.when(jnp.logical_and(last, jnp.logical_and(i >= 1, i < n + 1)))
        def _():
            lo_copy(i - 1).start()

        @pl.when(jnp.logical_and(last, jnp.logical_and(i >= 2, i < n)))
        def _():
            finish_swap(i - 2)

        @pl.when(live)
        def _():
            loop(2, t, lambda d: relay(t - d, i))

        j2 = i - back_lag
        @pl.when(jnp.logical_and(live, t > 1))
        def _():
            relay(0, i)

        @pl.when(jnp.logical_and(live, apart))
        def _():
            relay_other(i)

        @pl.when(live)
        def _():
            send_sums(i)

        @pl.when(jnp.logical_and(last, i == n - 1))
        def _():
            own_grad(i)

        @pl.when(jnp.logical_and(j2 >= 0, j2 < n))
        def _():
            backward(j2)

        @pl.when(jnp.logical_and(last, i == n))
        def _():
            loop(max(n - 2, 0), n, finish_swap)

        @pl.when(jnp.logical_and(last, i == n + sum_lag + 1))
        def _():
            loop(0, t + 1, dec_piece)

        j3 = i - sum_lag

        @pl.when(jnp.logical_and(below, jnp.logical_and(j3 >= 0, j3 < n)))
        def _():
            pass_on(j3)

        @pl.when(jnp.logical_and(below, jnp.logical_and(j3 >= 1, j3 <= n)))
        def _():
            combine(j3 - 1)

        @pl.when(jnp.logical_and(j3 >= 2, j3 <= n + 1))
        def _():
            masked(j3 - 2)

    loop(t + 1, layers, blank)
    loop(0, n + sum_lag + 2, step)

    for ref, sem in ((xg, x_ss), (rss, rs_ss), (og, og_ss)):
        settle(ref.at[departures], sem)
    for ref, sem in ((his, hi_ss), (los, lo_ss), (ys, y_ss)):
        settle(ref, sem)
    apart_rows = size * len(range(FROM, min(FROM + SWAPS, n)))

    @pl.when(last)
    def _():
        settle(bss, bs_ss)
        if apart_rows:
            settle(bss.at[pl.ds(0, apart_rows)], fs_ss)

    def drain(l):
        for h in range(2):
            less = jnp.logical_and(l == top - 1, y != h)

            @pl.when(jnp.logical_and(below, jnp.logical_not(less)))
            def _():
                settle(lat.at[l, h], zu_ss.at[l, h])

            @pl.when(jnp.logical_and(below, less))
            def _():
                settle(lat.at[l, h, pl.ds(0, size * n - apart_rows)], zu_ss.at[l, h])

            @pl.when(jnp.logical_and(last, jnp.logical_and(l < t, jnp.logical_not(less))))
            def _():
                settle(zds.at[l, h], zd_ss.at[l, h])

            if n > 1:
                @pl.when(jnp.logical_and(below, l < t))
                def _():
                    settle(zds.at[l, h, pl.ds(0, size * (n - 1))], zd_ss.at[l, h])

        @pl.when(jnp.logical_and(below, l < t))
        def _():
            settle(fas.at[l], fa_ss.at[l])

    loop(0, t + 1, drain)


def exchange(layer_inputs, mlp_outputs, enc_weight, enc_bias, dec_weight):
    layers, latents, width = dec_weight.shape
    blocks = lax.axis_size("latent")
    rb, depth = layer_inputs.shape
    rows = rb * blocks
    half = latents // 2
    rscale = rows ** (-0.5)
    chunks = next((c for c in CHUNKS if rb % (16 * c) == 0), 1)
    hbm = pl.BlockSpec(memory_space=pltpu.HBM)
    dma = pltpu.SemaphoreType.DMA
    per_chunk = dma((chunks,))
    one = dma
    per_layer = dma((layers - 1, chunks, 2))
    sides_sent = dma((layers - 1, 2))
    per_side = dma((chunks, 2))
    sides = pltpu.VMEM((2, rows, half), BF16)
    sent = pltpu.VMEM((layers, 2, rows, half), BF16)
    one_chunk = pltpu.VMEM((layers, 2, rows // chunks, half), BF16)
    return pl.pallas_call(
        functools.partial(exchange_kernel, layers, blocks, chunks, rscale),
        out_shape=(
            pltpu.VMEM((layers, latents, width), BF16),
            pltpu.VMEM((rows, depth), BF16),
            pltpu.VMEM((rows, latents), BF16),
        ),
        in_specs=[hbm] * 5,
        out_specs=(pl.BlockSpec(memory_space=pltpu.VMEM),) * 3,
        scratch_shapes=[
            pltpu.VMEM((rb, width), BF16),
            pltpu.VMEM((depth, latents), BF16),
            pltpu.VMEM((layers, latents), F32),
            pltpu.VMEM((layers, latents, width), BF16),
            pltpu.VMEM((2, rows, half), F32),
            sides, sides, sides, sides,
            sent,
            pltpu.VMEM((rows, width), F32),
            pltpu.VMEM((rows, width), BF16),
            pltpu.VMEM((blocks, rb, width), BF16),
            pltpu.VMEM((rows, width), BF16),
            pltpu.VMEM((layers, 2, rows, half), F32),
            sent, sent, sides, sides,
            pltpu.VMEM((rows, half), BF16), pltpu.VMEM((rows, half), BF16), one_chunk, one_chunk,
            one, per_chunk, one, per_side, one, per_chunk, sides_sent, per_layer,
            one, per_chunk, one, per_chunk, sides_sent, per_layer, one, per_side,
            one, per_chunk, one, per_chunk, dma((layers,)), dma((layers, 2)), one, dma((4,)),
        ],
        compiler_params=pltpu.CompilerParams(
            collective_id=0, has_side_effects=True, vmem_limit_bytes=40 * 2**20
        ),
        name="exchange",
    )(*(pltpu.with_memory_space_constraint(a, pltpu.HBM) for a in (layer_inputs, mlp_outputs, enc_weight, enc_bias, dec_weight)))


def finish_kernel(xg, pg, dec, enc_out, dec_out, enc, enc_sem, dec_sem):
    layers = dec.shape[0]
    piece = enc.shape[0] // layers
    writes = [pltpu.make_async_copy(dec.at[l], dec_out.at[l], dec_sem.at[l]) for l in range(layers)]
    for copy in writes:
        copy.start()
    for l in range(layers):
        part = pl.ds(l * piece, piece)
        enc[part, :] = lax.dot_general(
            xg[:, part], pg[...], (((0,), (0,)), ((), ())), preferred_element_type=F32
        )
        writes.append(pltpu.make_async_copy(enc.at[part], enc_out.at[part], enc_sem.at[l]))
        writes[-1].start()
    for copy in writes:
        copy.wait()


def local(layer_inputs, mlp_outputs, enc_weight, enc_bias, dec_weight):
    dec, xg, pg = exchange(layer_inputs, mlp_outputs, enc_weight, enc_bias, dec_weight)
    hbm = pl.BlockSpec(memory_space=pltpu.HBM)
    per_layer = pltpu.SemaphoreType.DMA((dec.shape[0],))
    return pl.pallas_call(
        finish_kernel,
        in_specs=[pl.BlockSpec(memory_space=pltpu.VMEM)] * 3,
        out_specs=(hbm,) * 2,
        out_shape=(
            jax.ShapeDtypeStruct(enc_weight.shape, F32),
            jax.ShapeDtypeStruct(dec_weight.shape, BF16),
        ),
        scratch_shapes=[pltpu.VMEM(enc_weight.shape, F32), per_layer, per_layer],
        compiler_params=pltpu.CompilerParams(vmem_limit_bytes=24 * 2**20),
        name="finish",
    )(xg, pg, dec)


def solution(mesh):
    in_specs = (
        P("latent", "layer"),
        P("latent", "layer"),
        P("layer", "latent"),
        P(None, "latent"),
        P(None, "latent", "layer"),
    )
    out_specs = (P("layer", "latent"), P(None, "latent", "layer"))
    return jax.shard_map(local, mesh=mesh, in_specs=in_specs, out_specs=out_specs, check_vma=False)
```

```python
import functools

import jax
import jax.numpy as jnp
from jax import lax
from jax.experimental import pallas as pl
from jax.experimental.pallas import tpu as pltpu
from jax.sharding import PartitionSpec as P

MESH = pl.DeviceIdType.MESH
F32 = jnp.float32
BF16 = jnp.bfloat16
CHUNKS = (6, 3, 2)
NEAR = 4
FROM = 2
SWAPS = 2


def exchange_kernel(
    layers, blocks, chunks, rscale,
    x_hbm, mlp_hbm, w_hbm, bias_hbm, v_hbm,
    dec, xg, pg,
    mlp, w, bias_all, v, pre, his, hir, los, lor, lat, recon, rss, rsr, og, acc, zds, zdr, ys, yr, bss, bsr, fas, far,
    x_ss, x_rs, hi_ss, hi_rs, lo_ss, lo_rs, zu_ss, zu_rs, rs_ss, rs_rs, og_ss, og_rs, zd_ss, zd_rs, y_ss, y_rs,
    fs_ss, fs_rs, bs_ss, bs_rs, fa_ss, fa_rs, own_sem, in_sem,
):
    p = lax.axis_index("layer")
    q = lax.axis_index("latent")
    t = p // 2
    y = p % 2
    n = chunks
    top = layers - 1
    last = t == top
    below = t < top
    near = t == top - 1
    s = x_hbm.shape[0] // n
    size = s * blocks
    half = w.shape[1] // 2
    partner = (p + 1 - 2 * y, q)
    up = (p + 2, q)
    down = (p - 2, q)
    chips = blocks // 2
    other = 1 - y

    def blk(k):
        return ((q // 2 + k // 2) % chips) * 2 + (q % 2 + k % 2) % 2

    def span(j):
        return pl.ds(pl.multiple_of(j * size, size), size)

    def piece(j, b):
        return pl.ds(pl.multiple_of(j * size + b * s, s), s)

    def mine(j):
        return pl.ds(pl.multiple_of(j * s, s), s)

    def rcopy(src, dst, ss, rs, dev):
        return pltpu.make_async_remote_copy(
            src_ref=src, dst_ref=dst, send_sem=ss, recv_sem=rs, device_id=dev, device_id_type=MESH
        )

    def loop(lower, upper, step):
        def body(i, carry):
            step(i)
            return carry

        lax.fori_loop(lower, upper, body, 0)

    def settle(ref, sem):
        pltpu.make_async_copy(ref, ref, sem).wait()

    def own_x(j):
        return pltpu.make_async_copy(x_hbm.at[mine(j)], xg.at[piece(j, q)], own_sem)

    w_copy = pltpu.make_async_copy(w_hbm, w, in_sem.at[0])
    bias_copy = pltpu.make_async_copy(bias_hbm, bias_all, in_sem.at[1])
    mlp_copy = pltpu.make_async_copy(mlp_hbm, mlp, in_sem.at[2])
    v_copy = pltpu.make_async_copy(v_hbm, v, in_sem.at[3])
    for j in range(n):
        own_x(j).start()
    for copy in (w_copy, bias_copy, mlp_copy, v_copy):
        copy.start()

    barrier = pltpu.get_barrier_semaphore()
    for k in range(1, blocks):
        pl.semaphore_signal(barrier, inc=1, device_id=(p, blk(k)), device_id_type=MESH)
    pl.semaphore_signal(barrier, inc=1, device_id=partner, device_id_type=MESH)

    @pl.when(below)
    def _():
        pl.semaphore_signal(barrier, inc=1, device_id=up, device_id_type=MESH)

    @pl.when(t > 0)
    def _():
        pl.semaphore_signal(barrier, inc=1, device_id=down, device_id_type=MESH)

    neighbours = blocks + below.astype(jnp.int32) + (t > 0).astype(jnp.int32)
    pl.semaphore_wait(barrier, neighbours)

    others = list(range(2, blocks)) + [1]

    def x_copy(j, k):
        part = xg.at[piece(j, q)]
        return rcopy(part, part, x_ss, x_rs.at[j], (p, blk(k)))

    def send_x(j):
        for k in others:
            x_copy(j, k).start()

    arrivals = pl.ds(0, (blocks - 1) * s)
    departures = pl.ds(0, (blocks - 1) * s * n)
    settle(xg.at[pl.ds(0, s * n)], own_sem)
    loop(0, n, send_x)

    def part_of(h):
        return pl.ds(pl.multiple_of(h * half, half), half)

    def side(h):
        return slice(h * half, (h + 1) * half)

    def hi_copy(j, h):
        return rcopy(his.at[h, span(j)], hir.at[h, span(j)], hi_ss, hi_rs.at[j, h], partner)

    def lo_copy(j):
        return rcopy(los.at[:, span(j)], lor.at[:, span(j)], lo_ss, lo_rs.at[j], partner)

    def encode(j):
        settle(xg.at[arrivals], x_rs.at[j])
        for h in range(2):
            part = jnp.dot(xg[span(j), :], w[:, side(h)], preferred_element_type=F32)
            pre[h, span(j)] = part
            hi = part.astype(BF16)
            his[h, span(j)] = hi
            hi_copy(j, h).start()
            los[h, span(j)] = (part - hi.astype(F32)).astype(BF16)

    def zu_copy(l, j, h):
        part = lat.at[l, h, span(j)]
        return rcopy(part, part, zu_ss.at[l, h], zu_rs.at[l, j, h], up)

    bias_copy.wait()
    own_row = lax.broadcasted_iota(jnp.int32, bias_all.shape, 0) == t
    bias = jnp.sum(jnp.where(own_row, bias_all[...], 0.0), axis=0, keepdims=True)
    w_copy.wait()
    ahead = jnp.where(last, n, min(n, 3))
    early = min(n, 2)
    loop(0, early, encode)

    def decoded(l, j):
        return jnp.dot(lat[l, 0, span(j)], v[l, :half, :], preferred_element_type=F32) + jnp.dot(
            lat[l, 1, span(j)], v[l, half:, :], preferred_element_type=F32
        )

    def swapped(l, j):
        return jnp.logical_and(l == top - 1, jnp.logical_and(j >= FROM, j < FROM + SWAPS))

    def goes_up(l, j, h):
        return jnp.logical_and(below, jnp.logical_or(jnp.logical_not(swapped(l, j)), y == h))

    def own_latents(j):
        for h in range(2):
            hi_copy(j, h).wait_recv()
            total = pre[h, span(j)] + hir[h, span(j)].astype(F32) + bias[:, side(h)]
            pre[h, span(j)] = total
            lat[t, h, span(j)] = jnp.maximum(total, 0.0).astype(BF16)

            @pl.when(goes_up(t, j, h))
            def _():
                zu_copy(t, j, h).start()

        @pl.when(below)
        def _():
            lo_copy(j).start()

    def relay(l, j):
        for h in range(2):
            zu_copy(l, j, h).wait_recv()

            @pl.when(below)
            def _():
                zu_copy(l, j, h).start()

        recon[span(j), :] += decoded(l, j)

    def fs_copy(j, h):
        part = lat.at[top - 1, h, span(j)]
        return rcopy(part, part, fs_ss, fs_rs.at[j], partner)

    def add_half(j, h):
        recon[span(j), :] += jnp.dot(lat[top - 1, h, span(j)], v[top - 1, part_of(h), :], preferred_element_type=F32)

    def swap_half(j):
        zu_copy(top - 1, j, y).wait_recv()
        fs_copy(j, y).start()
        add_half(j, y)

    def relay_other(j):
        fs_copy(j, other).wait_recv()
        add_half(j, other)

    def rs_copy(j, k):
        b = blk(k)
        return rcopy(rss.at[piece(j, b)], rsr.at[q, mine(j)], rs_ss, rs_rs.at[j], (p, b))

    def send_sums(j):
        rss[span(j), :] = recon[span(j), :].astype(BF16)
        for k in others:
            rs_copy(j, k).start()

    def og_copy(j, k):
        part = og.at[piece(j, q)]
        return rcopy(part, part, og_ss, og_rs.at[j], (p, blk(k)))

    def own_grad(j):
        total = recon[piece(j, q), :]
        settle(rss.at[arrivals], rs_rs.at[j])
        for k in range(1, blocks):
            total = total + rsr[blk(k), mine(j)].astype(F32)
        og[piece(j, q), :] = ((total - mlp[mine(j), :].astype(F32)) * rscale).astype(BF16)
        for k in others:
            og_copy(j, k).start()

    def zd_copy(l, j, h):
        return rcopy(zds.at[l, h, span(j)], zdr.at[l, h, span(j)], zd_ss.at[l, h], zd_rs.at[l, j, h], down)

    def y_copy(j, h):
        return rcopy(ys.at[h, span(j)], yr.at[h, span(j)], y_ss, y_rs.at[j, h], partner)

    def bs_copy(j):
        return rcopy(bss.at[span(j)], bsr.at[span(j)], bs_ss, bs_rs.at[j], partner)

    def back(l, j, h):
        return lax.dot_general(
            og[span(j), :], v[l, part_of(h), :], (((1,), (1,)), ((), ())), preferred_element_type=F32
        )

    def send_down(l, j, h, total):
        zds[l, h, span(j)] = total.astype(BF16)
        zd_copy(l, j, h).start()

    def far_copy(l, h):
        return rcopy(fas.at[l, h], far.at[t, h], fa_ss.at[l], fa_rs.at[t, h], (p - 2 * (t - l), q))

    def far_in(u, h):
        return rcopy(fas.at[t, h], far.at[u, h], fa_ss.at[t], fa_rs.at[u, h], (p + 2 * (u - t), q))

    def send_far(l, h, total):
        fas[l, h] = total.astype(BF16)
        far_copy(l, h).start()

    def send_across(j, h, total):
        acc[t, h, span(j)] = total
        ys[h, span(j)] = total.astype(BF16)
        y_copy(j, h).start()

    def send_own(j):
        for h in range(2):
            ys[h, span(j)] = acc[top, h, span(j)].astype(BF16)
            y_copy(j, h).start()

    def backward(j):
        settle(og.at[arrivals], og_rs.at[j])

        @pl.when(last)
        def _():
            def produce(l):
                for h in range(2):
                    send_down(l, j, h, back(l, j, h))

            loop(0, min(top - 1, 1), produce)
            bss[span(j)] = back(top - 1, j, other).astype(BF16)
            bs_copy(j).start()

            @pl.when(j > 0)
            def _():
                send_own(j - 1)

            loop(min(top - 1, 1), top - 1, produce)
            for h in range(2):
                acc[top, h, span(j)] = back(top, j, h)
            acc[top - 1, y, span(j)] = back(top - 1, j, y)

            @pl.when(j == n - 1)
            def _():
                send_own(j)

        @pl.when(below)
        def _():
            def keep(l):
                for h in range(2):
                    total = back(l, j, h)
                    alone = jnp.logical_and(jnp.logical_and(j == n - 1, l < t), jnp.logical_not(near))

                    @pl.when(alone)
                    def _():
                        send_far(l, h, total)

                    @pl.when(jnp.logical_not(alone))
                    def _():
                        acc[l, h, span(j)] = total

            loop(0, t + 1, keep)

            @pl.when(near)
            def _():
                send_across(j, other, acc[t, other, span(j)])

    def finish_swap(j):
        bs_copy(j).wait_recv()
        send_down(top - 1, j, y, acc[top - 1, y, span(j)] + bsr[span(j)].astype(F32))

    def summed(l, j, h):
        zd_copy(l, j, h).wait_recv()
        return acc[l, h, span(j)] + zdr[l, h, span(j)].astype(F32)

    def pass_on(j):
        final = j == n - 1

        def add(l):
            for h in range(2):
                @pl.when(jnp.logical_not(final))
                def _():
                    send_down(l, j, h, summed(l, j, h))

                @pl.when(jnp.logical_and(final, near))
                def _():
                    send_far(l, h, summed(l, j, h))

            @pl.when(final)
            def _():
                dec_piece(l)

        loop(0, t, add)

    def combine(j):
        final = j == n - 1

        @pl.when(near)
        def _():
            send_across(j, y, summed(t, j, y))

        @pl.when(jnp.logical_not(jnp.logical_or(near, final)))
        def _():
            for h in range(2):
                send_across(j, h, summed(t, j, h))

        @pl.when(jnp.logical_and(final, jnp.logical_not(near)))
        def _():
            for h in range(2):
                def add_far(u):
                    far_in(u, h).wait_recv()
                    acc[t, h, span(j)] += far[u, h].astype(F32)

                loop(t + 1, top, add_far)
                send_across(j, h, acc[t, h, span(j)])

        @pl.when(final)
        def _():
            dec_piece(t)

    def masked(j):
        lo_copy(j).wait_recv()
        for h in range(2):
            y_copy(j, h).wait_recv()
            active = pre[h, span(j)] + lor[h, span(j)].astype(F32) > 0.0
            total = acc[t, h, span(j)] + yr[h, span(j)].astype(F32)
            pg[span(j), side(h)] = jnp.where(active, total, 0.0).astype(BF16)

    def dec_piece(l):
        for h in range(2):
            part = lax.dot_general(lat[l, h], og[...], (((0,), (0,)), ((), ())), preferred_element_type=F32)
            dec[l, h * half:(h + 1) * half, :] = part.astype(BF16)

    def blank(l):
        dec[l] = jnp.zeros((2 * half, dec.shape[2]), BF16)

    grad_lag = jnp.where(last, 1, 2)
    back_lag = jnp.where(last, 1, 3)
    sum_lag = jnp.where(last, 1, jnp.where(near, NEAR, max(n - 1, NEAR)))
    own_latents(0)
    loop(early, ahead, encode)
    v_copy.wait()
    mlp_copy.wait()

    def step(i):
        live = i < n
        j = i - grad_lag
        soon = jnp.logical_and(last, j == n - 1)

        @pl.when(jnp.logical_and(jnp.logical_and(j >= 0, j < n), jnp.logical_not(soon)))
        def _():
            own_grad(j)

        @pl.when(i + 1 < n)
        def _():
            own_latents(i + 1)

        @pl.when(i + ahead < n)
        def _():
            encode(i + ahead)

        @pl.when(live)
        def _():
            recon[span(i), :] = decoded(t, i)

        apart = jnp.logical_and(last, swapped(t - 1, i))

        @pl.when(jnp.logical_and(live, jnp.logical_and(t > 0, jnp.logical_not(apart))))
        def _():
            relay(t - 1, i)

        @pl.when(jnp.logical_and(live, apart))
        def _():
            swap_half(i)

        @pl.when(jnp.logical_and(last, jnp.logical_and(i >= 1, i < n + 1)))
        def _():
            lo_copy(i - 1).start()

        @pl.when(jnp.logical_and(last, jnp.logical_and(i >= 2, i < n)))
        def _():
            finish_swap(i - 2)

        @pl.when(live)
        def _():
            loop(2, t, lambda d: relay(t - d, i))

        j2 = i - back_lag
        @pl.when(jnp.logical_and(live, t > 1))
        def _():
            relay(0, i)

        @pl.when(jnp.logical_and(live, apart))
        def _():
            relay_other(i)

        @pl.when(live)
        def _():
            send_sums(i)

        @pl.when(jnp.logical_and(last, i == n - 1))
        def _():
            own_grad(i)

        @pl.when(jnp.logical_and(j2 >= 0, j2 < n))
        def _():
            backward(j2)

        @pl.when(jnp.logical_and(last, i == n))
        def _():
            loop(max(n - 2, 0), n, finish_swap)

        @pl.when(jnp.logical_and(last, i == n + sum_lag + 1))
        def _():
            loop(0, t + 1, dec_piece)

        j3 = i - sum_lag

        @pl.when(jnp.logical_and(below, jnp.logical_and(j3 >= 0, j3 < n)))
        def _():
            pass_on(j3)

        @pl.when(jnp.logical_and(below, jnp.logical_and(j3 >= 1, j3 <= n)))
        def _():
            combine(j3 - 1)

        @pl.when(jnp.logical_and(j3 >= 2, j3 <= n + 1))
        def _():
            masked(j3 - 2)

    loop(t + 1, layers, blank)
    loop(0, n + sum_lag + 2, step)

    for ref, sem in ((xg, x_ss), (rss, rs_ss), (og, og_ss)):
        settle(ref.at[departures], sem)
    for ref, sem in ((his, hi_ss), (los, lo_ss), (ys, y_ss)):
        settle(ref, sem)
    apart_rows = size * len(range(FROM, min(FROM + SWAPS, n)))

    @pl.when(last)
    def _():
        settle(bss, bs_ss)
        if apart_rows:
            settle(bss.at[pl.ds(0, apart_rows)], fs_ss)

    def drain(l):
        for h in range(2):
            less = jnp.logical_and(l == top - 1, y != h)

            @pl.when(jnp.logical_and(below, jnp.logical_not(less)))
            def _():
                settle(lat.at[l, h], zu_ss.at[l, h])

            @pl.when(jnp.logical_and(below, less))
            def _():
                settle(lat.at[l, h, pl.ds(0, size * n - apart_rows)], zu_ss.at[l, h])

            @pl.when(jnp.logical_and(last, jnp.logical_and(l < t, jnp.logical_not(less))))
            def _():
                settle(zds.at[l, h], zd_ss.at[l, h])

            if n > 1:
                @pl.when(jnp.logical_and(below, l < t))
                def _():
                    settle(zds.at[l, h, pl.ds(0, size * (n - 1))], zd_ss.at[l, h])

        @pl.when(jnp.logical_and(below, l < t))
        def _():
            settle(fas.at[l], fa_ss.at[l])

    loop(0, t + 1, drain)


def exchange(layer_inputs, mlp_outputs, enc_weight, enc_bias, dec_weight):
    layers, latents, width = dec_weight.shape
    blocks = lax.axis_size("latent")
    rb, depth = layer_inputs.shape
    rows = rb * blocks
    half = latents // 2
    rscale = rows ** (-0.5)
    chunks = next((c for c in CHUNKS if rb % (16 * c) == 0), 1)
    hbm = pl.BlockSpec(memory_space=pltpu.HBM)
    dma = pltpu.SemaphoreType.DMA
    per_chunk = dma((chunks,))
    one = dma
    per_layer = dma((layers - 1, chunks, 2))
    sides_sent = dma((layers - 1, 2))
    per_side = dma((chunks, 2))
    sides = pltpu.VMEM((2, rows, half), BF16)
    sent = pltpu.VMEM((layers, 2, rows, half), BF16)
    one_chunk = pltpu.VMEM((layers, 2, rows // chunks, half), BF16)
    return pl.pallas_call(
        functools.partial(exchange_kernel, layers, blocks, chunks, rscale),
        out_shape=(
            pltpu.VMEM((layers, latents, width), BF16),
            pltpu.VMEM((rows, depth), BF16),
            pltpu.VMEM((rows, latents), BF16),
        ),
        in_specs=[hbm] * 5,
        out_specs=(pl.BlockSpec(memory_space=pltpu.VMEM),) * 3,
        scratch_shapes=[
            pltpu.VMEM((rb, width), BF16),
            pltpu.VMEM((depth, latents), BF16),
            pltpu.VMEM((layers, latents), F32),
            pltpu.VMEM((layers, latents, width), BF16),
            pltpu.VMEM((2, rows, half), F32),
            sides, sides, sides, sides,
            sent,
            pltpu.VMEM((rows, width), F32),
            pltpu.VMEM((rows, width), BF16),
            pltpu.VMEM((blocks, rb, width), BF16),
            pltpu.VMEM((rows, width), BF16),
            pltpu.VMEM((layers, 2, rows, half), F32),
            sent, sent, sides, sides,
            pltpu.VMEM((rows, half), BF16), pltpu.VMEM((rows, half), BF16), one_chunk, one_chunk,
            one, per_chunk, one, per_side, one, per_chunk, sides_sent, per_layer,
            one, per_chunk, one, per_chunk, sides_sent, per_layer, one, per_side,
            one, per_chunk, one, per_chunk, dma((layers,)), dma((layers, 2)), one, dma((4,)),
        ],
        compiler_params=pltpu.CompilerParams(
            collective_id=0, has_side_effects=True, vmem_limit_bytes=40 * 2**20
        ),
        name="exchange",
    )(*(pltpu.with_memory_space_constraint(a, pltpu.HBM) for a in (layer_inputs, mlp_outputs, enc_weight, enc_bias, dec_weight)))


def finish_kernel(xg, pg, dec, enc_out, dec_out, enc, enc_sem, dec_sem):
    layers = dec.shape[0]
    piece = enc.shape[0] // layers
    writes = [pltpu.make_async_copy(dec.at[l], dec_out.at[l], dec_sem.at[l]) for l in range(layers)]
    for copy in writes:
        copy.start()
    for l in range(layers):
        part = pl.ds(l * piece, piece)
        enc[part, :] = lax.dot_general(
            xg[:, part], pg[...], (((0,), (0,)), ((), ())), preferred_element_type=F32
        )
        writes.append(pltpu.make_async_copy(enc.at[part], enc_out.at[part], enc_sem.at[l]))
        writes[-1].start()
    for copy in writes:
        copy.wait()


def local(layer_inputs, mlp_outputs, enc_weight, enc_bias, dec_weight):
    dec, xg, pg = exchange(layer_inputs, mlp_outputs, enc_weight, enc_bias, dec_weight)
    hbm = pl.BlockSpec(memory_space=pltpu.HBM)
    per_layer = pltpu.SemaphoreType.DMA((dec.shape[0],))
    return pl.pallas_call(
        finish_kernel,
        in_specs=[pl.BlockSpec(memory_space=pltpu.VMEM)] * 3,
        out_specs=(hbm,) * 2,
        out_shape=(
            jax.ShapeDtypeStruct(enc_weight.shape, F32),
            jax.ShapeDtypeStruct(dec_weight.shape, BF16),
        ),
        scratch_shapes=[pltpu.VMEM(enc_weight.shape, F32), per_layer, per_layer],
        compiler_params=pltpu.CompilerParams(vmem_limit_bytes=24 * 2**20),
        name="finish",
    )(xg, pg, dec)


def solution(mesh):
    in_specs = (
        P("latent", "layer"),
        P("latent", "layer"),
        P("layer", "latent"),
        P(None, "latent"),
        P(None, "latent", "layer"),
    )
    out_specs = (P("layer", "latent"), P(None, "latent", "layer"))
    return jax.shard_map(local, mesh=mesh, in_specs=in_specs, out_specs=out_specs, check_vma=False)
```
